128 devices in a mesh: dp: 8 (over z, core), sp: 16 (over y, x).
Axes of the slice: x: 4, y: 4, z: 4, core: 2. Of those that a mesh axis runs over, the one named last changes fastest.
Arguments:
- projected: bfloat16 [16384, 10240], P(('dp', 'sp')), may hold values from -4 to 4
- bias: float32 [10240], replicated, may hold values from -3 to 3
- cotangent: bfloat16 [16384, 8192], P(('dp', 'sp')), may hold values from -4 to 4
- lengths: int32 [8, 4], P('dp'), may hold values from 1 to 1024, 2048 in all within a row
- page_source: int32 [8, 128], P('dp'), may hold values from 0 to 127, as said below
Outputs:
- attended: bfloat16 [16384, 8192], P(('dp', 'sp'))
- grad_query: bfloat16 [16384, 8192], P(('dp', 'sp'))
- key_value_gradient: bfloat16 [16384, 2048], P(('dp', 'sp'))
- grad_bias: float32 [10240], replicated
The draws below stay inside these ranges and needn't reach their ends.
Inputs may be any that keep to these rules, and one draw needn't show every extreme that they name: Each row holds the lengths of the 4 sequences of one group in packed order and sums to 2048; the longest is exactly 1024. `page_source`: rollout page r of a group lies on the group's device r // 8 at slot r % 8. Each row is a permutation of the group's pages, and no device sends two pages to the same device of its group.
All inputs are finite; a program needn't handle non-finite values.
Results may differ from the reference program's by a relative error of at most 0.012.
Values may be sent and summed in bfloat16 or wider, within the bound.
No kernel may reach another device: no remote copies, remote signals or barrier semaphores. Data moves between devices by JAX's collectives and lax.ppermute only.
A program may use at most 192 MiB of HBM per device.

```python
import math
import jax
import jax.numpy as jnp
import numpy as np
from jax import lax

QUERY_HEADS = 64
KEY_VALUE_HEADS = 8
HEAD_DIMENSION = 128
TOK_DEV = 128
SEQS = 4
PAGE = 16
GROUPS = 8
GROUP = 2048
TOKENS = 16384
WIDTH = 10240


def draw_page_source(key, part):
    pages_dev = TOK_DEV // PAGE
    devices = GROUP // TOK_DEV

    def one_group(subkey):
        first_key, second_key, third_key = jax.random.split(subkey, 3)
        device_order = jax.random.permutation(first_key, devices).astype(jnp.int32)
        shifts = jax.random.permutation(second_key, devices)[:pages_dev].astype(jnp.int32)
        slot_order = jax.random.permutation(third_key, pages_dev).astype(jnp.int32)
        target = jnp.arange(devices, dtype=jnp.int32)[:, None]
        source = device_order[(target + shifts[None, :]) % devices]
        place = (slot_order[None, :] + source) % pages_dev
        return (source * pages_dev + place).reshape(devices * pages_dev).astype(jnp.int32)
    return jax.vmap(one_group)(jax.random.split(jax.random.fold_in(key, 17), GROUPS))


def levels(stream_key, dims, shards, least, largest):
    def one(dim, blocks):
        draws = jax.random.uniform(jax.random.fold_in(jax.random.fold_in(stream_key, 6), dim), (blocks,), jnp.float32, least / len(shards), largest / len(shards))
        return jnp.repeat(jnp.exp(draws), dims[dim] // blocks).reshape((-1,) + (1,) * (len(dims) - dim - 1))

    loudness = one(*shards[0])
    for cut in shards[1:]:
        loudness = loudness * one(*cut)
    return loudness


def length_profile(amount, total, limit, skew):
    portions = [(1 << 20) // math.isqrt(grade ** skew) + 1 for grade in range(2, amount + 1)]
    spare, holding = total - limit - (amount - 1), [1] * (amount - 1)
    while spare > 0:
        candidates = [i for i in range(amount - 1) if holding[i] < limit]
        mass, remaining = sum([portions[i] for i in candidates]), spare
        for i in candidates:
            addition = min(limit - holding[i], max(1, remaining * portions[i] // mass), spare)
            holding[i] = holding[i] + addition
            spare = spare - addition
    return np.array([limit] + holding)


def ragged_sizes(own_key, number_of, total, limit, slope):
    if number_of == 2:
        one = jax.random.randint(own_key, (), max(1, total - limit), min(limit, total - 1) + 1)
        return jnp.stack([one, total - one])
    sizes = jnp.asarray(length_profile(number_of, total, limit, slope), jnp.int32)
    couples = (number_of - 1) // 2
    source_of, sink = sizes[1:1 + 2 * couples:2], sizes[2:2 + 2 * couples:2]
    room = jnp.minimum(source_of - 1, limit - sink)
    passed = jax.random.randint(jax.random.fold_in(own_key, 1), (couples,), 0, 1 << 20) % (room + 1)
    sizes = sizes.at[1:1 + 2 * couples:2].set(source_of - passed).at[2:2 + 2 * couples:2].set(sink + passed)
    return sizes[jax.random.permutation(jax.random.fold_in(own_key, 2), number_of)]


def noise(own_key, dims, spread, reach, cuts=(), held_as=jnp.bfloat16):
    entries = jax.random.normal(own_key, dims, jnp.float32) * spread
    if len(cuts) > 0:
        entries = levels(own_key, dims, cuts, -0.22, 0.18) * entries
    return jnp.clip(entries, min=-reach, max=reach).astype(held_as)


def setup_inputs(seed: int = 0) -> dict:
    streams_of = jax.random.split(jax.random.key(seed), 6)
    return {
        "projected": noise(streams_of[0], (TOKENS, WIDTH), 1.0, 4.0, ((0, 128),)),
        "bias": noise(streams_of[1], (WIDTH,), 0.5, 3.0, (), jnp.float32),
        "cotangent": noise(streams_of[2], (TOKENS, QUERY_HEADS * HEAD_DIMENSION), 1.0, 4.0, ((0, 128),)),
        "lengths": jax.vmap(lambda own: ragged_sizes(own, SEQS, GROUP, GROUP // 2, 2))(jax.random.split(streams_of[3], GROUPS)).reshape((GROUPS, SEQS)).astype(jnp.int32),
        "page_source": draw_page_source(jax.random.fold_in(streams_of[5], 71), 0),
    }


rope_base = 1000000.0


def rope_tables(positions, head_size):
    half_size = head_size // 2
    exponent = jnp.arange(half_size, dtype=jnp.float32) * 2.0 / head_size
    frequency = jnp.power(jnp.float32(rope_base), -exponent)
    angles = positions.astype(jnp.float32)[:, None] * frequency[None, :]
    cosine_table = jnp.cos(angles)
    sine_table = jnp.sin(angles)
    return jnp.concatenate([cosine_table, cosine_table], 1), jnp.concatenate([sine_table, sine_table], 1)


def turn_half(tensor_in):
    half_size = tensor_in.shape[-1] // 2
    return jnp.concatenate([-tensor_in[..., half_size:], tensor_in[..., :half_size]], -1)


def apply_rotary(tensor_in, cosine_table, sine_table):
    return tensor_in * cosine_table[:, None, :] + turn_half(tensor_in) * sine_table[:, None, :]


def unrotate(tensor_in, cosine_table, sine_table):
    return tensor_in * cosine_table[:, None, :] - turn_half(tensor_in) * sine_table[:, None, :]


def segments_of(seq_lengths, token_total_count):
    seq_ends = jnp.cumsum(seq_lengths).astype(jnp.int32)
    seq_starts = seq_ends - seq_lengths
    tokens_at = jnp.arange(token_total_count, dtype=jnp.int32)
    segment = jnp.sum((tokens_at[:, None] >= seq_ends[None, :]).astype(jnp.int32), 1)
    labels = jnp.arange(seq_lengths.shape[0], dtype=jnp.int32)
    first_token = jnp.sum(jnp.where(segment[:, None] == labels[None, :], seq_starts[None, :], 0), 1)
    return segment, tokens_at - first_token, first_token


def rounded_duplicate(tensor_in):
    return lax.optimization_barrier(tensor_in.astype(jnp.bfloat16))


def attend_head(inputs, keep):
    query_rows, key_rows, value_rows, upstream_gradient = inputs
    score_scale = HEAD_DIMENSION ** -0.5
    query_wide = query_rows.astype(jnp.float32)
    key_wide = key_rows.astype(jnp.float32)
    value_wide = value_rows.astype(jnp.float32)
    upstream_wide = upstream_gradient.astype(jnp.float32)
    scores = jnp.einsum("qgd,kd->gqk", query_wide, key_wide) * score_scale
    weights = jnp.where(keep[None], jnp.exp(scores), 0.0)
    totals = jnp.sum(weights, 2)
    probs = weights / totals[:, :, None]
    rounded = rounded_duplicate(probs).astype(jnp.float32)
    attended = rounded_duplicate(jnp.einsum("gqk,kd->qgd", rounded, value_wide))
    delta = jnp.transpose(jnp.sum(upstream_wide * attended.astype(jnp.float32), 2))
    dprobs = jnp.einsum("qgd,kd->gqk", upstream_wide, value_wide)
    dscores = rounded_duplicate(probs * (dprobs - delta[:, :, None])).astype(jnp.float32)
    rot_query = jnp.einsum("gqk,kd->qgd", dscores, key_wide) * score_scale
    rot_key = jnp.einsum("gqk,qgd->kd", dscores, query_wide) * score_scale
    grad_value = jnp.einsum("gqk,qgd->kd", rounded, upstream_wide)
    return attended, rot_query, rot_key, grad_value


def one_group(inputs, bias):
    rows_in, upstream_gradient, seq_lengths, page_table = inputs
    token_total_count = rows_in.shape[0]
    row_width = rows_in.shape[1]
    query_span_width = QUERY_HEADS * HEAD_DIMENSION
    key_value_width = KEY_VALUE_HEADS * HEAD_DIMENSION
    heads_per_group = QUERY_HEADS // KEY_VALUE_HEADS
    packed = rows_in.reshape(token_total_count // PAGE, PAGE, row_width)[page_table].reshape(token_total_count, row_width)
    segment, position, first_token = segments_of(seq_lengths, token_total_count)
    cosine_table, sine_table = rope_tables(position, HEAD_DIMENSION)
    query_matrix = packed[:, :query_span_width].astype(jnp.float32) + bias[:query_span_width]
    query_matrix = rounded_duplicate(apply_rotary(query_matrix.reshape(token_total_count, QUERY_HEADS, HEAD_DIMENSION), cosine_table, sine_table))
    every_key = packed[:, query_span_width:query_span_width + key_value_width].astype(jnp.float32) + bias[query_span_width:query_span_width + key_value_width]
    every_key = rounded_duplicate(apply_rotary(every_key.reshape(token_total_count, KEY_VALUE_HEADS, HEAD_DIMENSION), cosine_table, sine_table))
    every_value = rounded_duplicate(packed[:, query_span_width + key_value_width:].astype(jnp.float32) + bias[query_span_width + key_value_width:])
    every_value = every_value.reshape(token_total_count, KEY_VALUE_HEADS, HEAD_DIMENSION)
    tokens_at = jnp.arange(token_total_count, dtype=jnp.int32)
    keep = (segment[:, None] == segment[None, :]) & (tokens_at[:, None] >= tokens_at[None, :])
    head_inputs = (
        jnp.transpose(query_matrix.reshape(token_total_count, KEY_VALUE_HEADS, heads_per_group, HEAD_DIMENSION), (1, 0, 2, 3)),
        jnp.transpose(every_key, (1, 0, 2)),
        jnp.transpose(every_value, (1, 0, 2)),
        jnp.transpose(upstream_gradient.reshape(token_total_count, KEY_VALUE_HEADS, heads_per_group, HEAD_DIMENSION), (1, 0, 2, 3)),
    )
    attended, rot_query, rot_key, grad_value = lax.map(lambda item: attend_head(item, keep), head_inputs)
    attended = jnp.transpose(attended, (1, 0, 2, 3)).reshape(token_total_count, query_span_width)
    rot_query = jnp.transpose(rot_query, (1, 0, 2, 3)).reshape(token_total_count, QUERY_HEADS, HEAD_DIMENSION)
    grad_query = unrotate(rot_query, cosine_table, sine_table).astype(jnp.bfloat16).reshape(token_total_count, query_span_width)
    grad_key = unrotate(jnp.transpose(rot_key, (1, 0, 2)), cosine_table, sine_table).reshape(token_total_count, key_value_width)
    grad_value = jnp.transpose(grad_value, (1, 0, 2)).reshape(token_total_count, key_value_width)
    key_value_gradient = jnp.concatenate([grad_key, grad_value], 1).astype(jnp.bfloat16)
    return attended, grad_query, key_value_gradient


def reference(projected, bias, cotangent, lengths, page_source):
    group_count = lengths.shape[0]
    token_total_count = projected.shape[0] // group_count
    inputs = (
        projected.reshape(group_count, token_total_count, projected.shape[1]),
        cotangent.reshape(group_count, token_total_count, cotangent.shape[1]),
        lengths,
        page_source,
    )
    attended, grad_query, key_value_gradient = lax.map(lambda item: one_group(item, bias), inputs)
    attended = attended.reshape(projected.shape[0], QUERY_HEADS * HEAD_DIMENSION)
    grad_query = grad_query.reshape(projected.shape[0], QUERY_HEADS * HEAD_DIMENSION)
    key_value_gradient = key_value_gradient.reshape(projected.shape[0], 2 * KEY_VALUE_HEADS * HEAD_DIMENSION)
    grad_bias = jnp.concatenate([jnp.sum(grad_query.astype(jnp.float32), 0), jnp.sum(key_value_gradient.astype(jnp.float32), 0)])
    return attended, grad_query, key_value_gradient, grad_bias
```

```python
import functools

import jax
import jax.numpy as jnp
from jax import lax
from jax.experimental import pallas as pl
from jax.experimental.pallas import tpu as pltpu
from jax.sharding import PartitionSpec as P

QUERY_HEADS = 64
KEY_VALUE_HEADS = 8
HEAD = 128
PAGE = 16
BLK = 256
SCALE = HEAD ** (-0.5)
LOG2E = 1.4426950408889634
NEG = -1e30
ROPE_BASE = 1000000.0
VMEM_BYTES = 60 * 1024 * 1024
EXTRA = 8

BF = jnp.bfloat16
F32 = jnp.float32
ANY = pl.BlockSpec(memory_space=pl.ANY)
VM = pl.BlockSpec(memory_space=pltpu.VMEM)
SM = pl.BlockSpec(memory_space=pltpu.SMEM)


def params():
    return pltpu.CompilerParams(vmem_limit_bytes=VMEM_BYTES)


def cost(flops, nbytes):
    return pl.CostEstimate(flops=flops, bytes_accessed=nbytes, transcendentals=0)


def run_copies(copies):
    for copy in copies:
        copy.start()
    for copy in copies:
        copy.wait()


def pack_kernel(chunk, ways, proj, cot, out, sem):
    kv0 = QUERY_HEADS * HEAD
    copies = []

    def add(src, dst):
        copies.append(pltpu.make_async_copy(src, dst, sem.at[len(copies)]))

    copies_of = ways // KEY_VALUE_HEADS
    for d in range(ways):
        col = d * 512 + chunk * 256
        add(proj.at[:, pl.ds(col, 256)], out.at[d, :, pl.ds(0, 256)])
        add(cot.at[:, pl.ds(col, 256)], out.at[d, :, pl.ds(256, 256)])
        if chunk == 0:
            kcol = kv0 + (d // copies_of) * HEAD
            vcol = kcol + KEY_VALUE_HEADS * HEAD
            add(proj.at[:, pl.ds(kcol, HEAD)], out.at[d, :, pl.ds(512, HEAD)])
            add(proj.at[:, pl.ds(vcol, HEAD)], out.at[d, :, pl.ds(640, HEAD)])
    run_copies(copies)


def pack(chunk, ways, proj, cot):
    rows = proj.shape[0]
    width = 768 if chunk == 0 else 512
    return pl.pallas_call(
        functools.partial(pack_kernel, chunk, ways),
        out_shape=jax.ShapeDtypeStruct((ways, rows, width), BF),
        in_specs=[ANY, ANY],
        out_specs=VM,
        scratch_shapes=[pltpu.SemaphoreType.DMA((ways * (4 if chunk == 0 else 2),))],
        compiler_params=params(),
        cost_estimate=cost(0, 4 * ways * rows * width),
        name=f"pack{chunk}",
    )(proj, cot)


def rope(x, c, s):
    return x * c + pltpu.roll(x, HEAD // 2, 1) * s


def unrope(g, c, s):
    return g * c - pltpu.roll(g, HEAD // 2, 1) * s


def keys_kernel(page, kv, bias, cos, sin, k_out, v_out, kt_out, vt_out):
    kb = bias[0:1, :]
    vb = bias[1:2, :]
    npages = kv.shape[0] // PAGE

    def one(p, _):
        src = pl.ds(pl.multiple_of(page[p] * PAGE, PAGE), PAGE)
        dst = pl.ds(pl.multiple_of(p * PAGE, PAGE), PAGE)
        k = kv[src, 0:HEAD].astype(F32) + kb
        v = kv[src, HEAD : 2 * HEAD].astype(F32) + vb
        k_out[dst, :] = rope(k, cos[dst, :], sin[dst, :]).astype(BF)
        v_out[dst, :] = v.astype(BF)
        return 0

    lax.fori_loop(0, npages, one, 0, unroll=4)

    def turn(b, _):
        rows = pl.ds(pl.multiple_of(b * BLK, BLK), BLK)
        kt_out[:, rows] = jnp.transpose(k_out[rows, :].astype(F32)).astype(BF)
        vt_out[:, rows] = jnp.transpose(v_out[rows, :].astype(F32)).astype(BF)
        return 0

    lax.fori_loop(0, kv.shape[0] // BLK, turn, 0)


def make_keys(page, recv, bias, cos, sin):
    n = recv.shape[0]
    row = jax.ShapeDtypeStruct((n, HEAD), BF)
    col = jax.ShapeDtypeStruct((HEAD, n), BF)
    return pl.pallas_call(
        keys_kernel,
        grid=(1,),
        out_shape=(row, row, col, col),
        in_specs=[
            SM,
            pl.BlockSpec((n, 256), lambda i: (0, 2)),
            VM,
            VM,
            VM,
        ],
        out_specs=(VM, VM, VM, VM),
        compiler_params=params(),
        cost_estimate=cost(4 * 10**9, 6 * n * 256),
        name="keys",
    )(page, recv, bias, cos, sin)


def attend_kernel(
    last, first_block, page, qd, k, v, kt, vt, cos, sin, first, qbias, dk_in, dv_in, sums_in,
    out, dk, dv, sums, qs, st, ot, dqt,
):
    n = k.shape[0]
    blocks = n // BLK
    per = BLK // 128
    bias = [qbias[0:1, :], qbias[1:2, :]]

    def gather(p, _):
        src = pl.ds(pl.multiple_of(page[p] * PAGE, PAGE), PAGE)
        dst = pl.ds(pl.multiple_of(p * PAGE, PAGE), PAGE)
        c, s = cos[dst, :], sin[dst, :]
        base = (p // (BLK // PAGE)) * (2 * BLK) + (p % (BLK // PAGE)) * PAGE
        for h in range(2):
            x = qd[src, h * HEAD : (h + 1) * HEAD].astype(F32) + bias[h]
            qs[pl.ds(pl.multiple_of(base + h * BLK, PAGE), PAGE), :] = rope(x, c, s).astype(BF)
        return 0

    lax.fori_loop(0, n // PAGE, gather, 0, unroll=4)
    if last:
        dk[...] = dk_in[...]
        dv[...] = dv_in[...]
    else:
        dk[...] = jnp.zeros_like(dk)
        dv[...] = jnp.zeros_like(dv)

    nt = (((1,), (1,)), ((), ()))
    nn = (((1,), (0,)), ((), ()))

    def block(i, carry):
        rows = pl.ds(pl.multiple_of(i * BLK, BLK), BLK)
        q = qs[pl.ds(pl.multiple_of(i * 2 * BLK, 2 * BLK), 2 * BLK), :]
        do = jnp.concatenate([qd[rows, 256:384], qd[rows, 384:512]], 0)
        lo = first_block[i]
        start1 = first[0:1, rows]
        start = jnp.concatenate([start1, start1], 1)
        lane = lax.broadcasted_iota(jnp.int32, (1, BLK), 1) + i * BLK
        token = jnp.concatenate([lane, lane], 1)

        def score(j, m):
            cols = pl.ds(pl.multiple_of(j * BLK, BLK), BLK)
            s = lax.dot_general(k[cols, :], q, nt, preferred_element_type=F32) * (SCALE * LOG2E)
            key = lax.broadcasted_iota(jnp.int32, (BLK, 2 * BLK), 0) + j * BLK
            s = jnp.where((key <= token) & (key >= start), s, NEG)
            st[j - lo] = s
            return jnp.maximum(m, jnp.max(s, 0, keepdims=True))

        m = lax.fori_loop(lo, i + 1, score, jnp.full((1, 2 * BLK), NEG, F32))

        def expo(j, total):
            e = jnp.exp2(st[j - lo] - m)
            st[j - lo] = e
            return total + jnp.sum(e, 0, keepdims=True)

        total = lax.fori_loop(lo, i + 1, expo, jnp.zeros((1, 2 * BLK), F32))
        inv = 1.0 / total
        ot[...] = jnp.zeros_like(ot)

        def value(j, _):
            cols = pl.ds(pl.multiple_of(j * BLK, BLK), BLK)
            p = st[j - lo] * inv
            st[j - lo] = p
            ot[...] += lax.dot_general(vt[:, cols], p.astype(BF), nn, preferred_element_type=F32)
            return 0

        lax.fori_loop(lo, i + 1, value, 0)
        o_t = ot[...].astype(BF).astype(F32)
        do_t = jnp.transpose(do.astype(F32))
        delta = jnp.sum(o_t * do_t, 0, keepdims=True)
        dqt[...] = jnp.zeros_like(dqt)

        def back(j, _):
            cols = pl.ds(pl.multiple_of(j * BLK, BLK), BLK)
            p = st[j - lo]
            dp = lax.dot_general(v[cols, :], do, nt, preferred_element_type=F32)
            ds = (p * (dp - delta)).astype(BF)
            dv[cols, :] += lax.dot_general(p.astype(BF), do, nn, preferred_element_type=F32)
            dk[cols, :] += lax.dot_general(ds, q, nn, preferred_element_type=F32)
            dqt[...] += lax.dot_general(kt[:, cols], ds, nn, preferred_element_type=F32)
            return 0

        lax.fori_loop(lo, i + 1, back, 0)
        o = jnp.transpose(o_t).astype(BF)
        dq = jnp.transpose(dqt[...]) * SCALE
        c, s = cos[rows, :], sin[rows, :]
        new = []
        for h in range(2):
            g = unrope(dq[h * BLK : (h + 1) * BLK], c, s).astype(BF)
            new.append(carry[h] + jnp.sum(g.astype(F32), 0, keepdims=True))
            for a in range(per):
                part = slice(a * 128, (a + 1) * 128)
                out[i * per + a, 0:128, h * HEAD : (h + 1) * HEAD] = o[h * BLK + a * 128 : h * BLK + (a + 1) * 128]
                out[i * per + a, 0:128, 256 + h * HEAD : 256 + (h + 1) * HEAD] = g[part]
        return tuple(new)

    zero = jnp.zeros((1, HEAD), F32)
    head_sums = lax.fori_loop(0, blocks, block, (zero, zero))
    if not last:
        sums[...] = jnp.zeros_like(sums)
        sums[0:1, :] = head_sums[0]
        sums[1:2, :] = head_sums[1]
        return

    def finish(b, carry):
        rows = pl.ds(pl.multiple_of(b * 128, 128), 128)
        gk = unrope(dk[rows, :] * SCALE, cos[rows, :], sin[rows, :])
        gv = dv[rows, :]
        out[b, 0:128, 512:640] = gk.astype(BF)
        out[b, 0:128, 640:768] = gv.astype(BF)
        return (
            carry[0] + jnp.sum(gk, 0, keepdims=True),
            carry[1] + jnp.sum(gv, 0, keepdims=True),
        )

    kv_sums = lax.fori_loop(0, n // 128, finish, (zero, zero))
    sums[...] = sums_in[...]
    sums[2:3, :] = head_sums[0]
    sums[3:4, :] = head_sums[1]
    sums[4:5, :] = kv_sums[0]
    sums[5:6, :] = kv_sums[1]


def attend(last, ways, first_block, page, recv, keys, cos, sin, first, qbias, dk, dv, sums):
    n = recv.shape[0]
    k, v, kt, vt = keys
    rows, width = (128 + EXTRA, 768) if last else (128, 512)
    grad = jax.ShapeDtypeStruct((n, HEAD), F32)
    return pl.pallas_call(
        functools.partial(attend_kernel, last),
        grid=(1,),
        out_shape=(
            jax.ShapeDtypeStruct((ways, rows, width), BF),
            grad,
            grad,
            jax.ShapeDtypeStruct((8, HEAD), F32),
        ),
        in_specs=[SM, SM, pl.BlockSpec((n, 512), lambda i: (0, 0))] + [VM] * 11,
        out_specs=(VM, VM, VM, VM),
        scratch_shapes=[
            pltpu.VMEM((2 * n, HEAD), BF),
            pltpu.VMEM((1024 // BLK + 1, BLK, 2 * BLK), F32),
            pltpu.VMEM((HEAD, 2 * BLK), F32),
            pltpu.VMEM((HEAD, 2 * BLK), F32),
        ],
        compiler_params=params(),
        cost_estimate=cost(20 * 10**9, 10**7),
        name="attend1" if last else "attend0",
    )(first_block, page, recv, k, v, kt, vt, cos, sin, first, qbias, dk, dv, sums)


def sums_kernel(sums, _, out, rows, sem):
    for r in range(6):
        x = sums[r : r + 1, :]
        hi = x.astype(BF).astype(F32)
        mid = (x - hi).astype(BF).astype(F32)
        low = x - hi - mid
        rows[:, r * HEAD : (r + 1) * HEAD] = jnp.concatenate(
            [hi, mid, low, jnp.zeros((EXTRA - 3, HEAD), F32)], 0
        ).astype(BF)
    run_copies(
        [
            pltpu.make_async_copy(rows, out.at[d, pl.ds(128, EXTRA), :], sem.at[d])
            for d in range(out.shape[0])
        ]
    )


def put_sums(sums, payload):
    ways = payload.shape[0]
    return pl.pallas_call(
        sums_kernel,
        out_shape=jax.ShapeDtypeStruct(payload.shape, payload.dtype),
        in_specs=[VM, ANY],
        out_specs=ANY,
        input_output_aliases={1: 0},
        scratch_shapes=[pltpu.VMEM((EXTRA, 768), BF), pltpu.SemaphoreType.DMA((ways,))],
        compiler_params=params(),
        name="sums",
    )(sums, payload)


def unpack0_kernel(recv, att, gq, sem):
    copies = []
    for d in range(recv.shape[0]):
        cols = pl.ds(d * 512, 256)
        copies.append(pltpu.make_async_copy(recv.at[d, :, pl.ds(0, 256)], att.at[:, cols], sem.at[2 * d]))
        copies.append(pltpu.make_async_copy(recv.at[d, :, pl.ds(256, 256)], gq.at[:, cols], sem.at[2 * d + 1]))
    run_copies(copies)


def unpack0(recv):
    ways, rows, _ = recv.shape
    shape = jax.ShapeDtypeStruct((rows, QUERY_HEADS * HEAD), BF)
    return pl.pallas_call(
        unpack0_kernel,
        out_shape=(shape, shape),
        in_specs=[VM],
        out_specs=(ANY, ANY),
        scratch_shapes=[pltpu.SemaphoreType.DMA((2 * ways,))],
        compiler_params=params(),
        cost_estimate=cost(0, 4 * ways * rows * 512),
        name="unpack0",
    )(recv)


def unpack1_kernel(recv, _a, _g, att, gq, kvg, gb, sem):
    copies = []
    ways = recv.shape[0]
    for d in range(ways):
        cols = pl.ds(d * 512 + 256, 256)
        copies.append(
            pltpu.make_async_copy(recv.at[d, pl.ds(0, 128), pl.ds(0, 256)], att.at[:, cols], sem.at[2 * d])
        )
        copies.append(
            pltpu.make_async_copy(recv.at[d, pl.ds(0, 128), pl.ds(256, 256)], gq.at[:, cols], sem.at[2 * d + 1])
        )
    for copy in copies:
        copy.start()
    share = ways // KEY_VALUE_HEADS
    qw = QUERY_HEADS * HEAD
    kw = KEY_VALUE_HEADS * HEAD

    def sums_of(d):
        t = recv[d, 128 : 128 + EXTRA, :].astype(F32)
        return t[0:1] + t[1:2] + t[2:3]

    for h in range(KEY_VALUE_HEADS):
        grad = jnp.zeros((128, 256), F32)
        kvsum = jnp.zeros((1, 256), F32)
        for r in range(share):
            d = h * share + r
            grad = grad + recv[d, 0:128, 512:768].astype(F32)
            b = sums_of(d)
            gb[:, d * 512 : (d + 1) * 512] = b[:, 0:512]
            kvsum = kvsum + b[:, 512:768]
        kvg[:, h * HEAD : (h + 1) * HEAD] = grad[:, :HEAD].astype(BF)
        kvg[:, kw + h * HEAD : kw + (h + 1) * HEAD] = grad[:, HEAD:].astype(BF)
        gb[:, qw + h * HEAD : qw + (h + 1) * HEAD] = kvsum[:, :HEAD]
        gb[:, qw + kw + h * HEAD : qw + kw + (h + 1) * HEAD] = kvsum[:, HEAD:]
    for copy in copies:
        copy.wait()


def unpack1(recv, att, gq):
    ways = recv.shape[0]
    rows = att.shape[0]
    return pl.pallas_call(
        unpack1_kernel,
        out_shape=(
            jax.ShapeDtypeStruct(att.shape, BF),
            jax.ShapeDtypeStruct(gq.shape, BF),
            jax.ShapeDtypeStruct((rows, 2 * KEY_VALUE_HEADS * HEAD), BF),
            jax.ShapeDtypeStruct((1, (QUERY_HEADS + 2 * KEY_VALUE_HEADS) * HEAD), F32),
        ),
        in_specs=[VM, ANY, ANY],
        out_specs=(ANY, ANY, VM, VM),
        input_output_aliases={1: 0, 2: 1},
        scratch_shapes=[pltpu.SemaphoreType.DMA((2 * ways,))],
        compiler_params=params(),
        cost_estimate=cost(0, 4 * ways * rows * 768),
        name="unpack1",
    )(recv, att, gq)


def rope_tables(positions):
    lane = jnp.arange(HEAD, dtype=jnp.int32)
    exponent = (lane % (HEAD // 2)).astype(F32) * 2.0 / HEAD
    frequency = jnp.power(jnp.float32(ROPE_BASE), -exponent)
    angles = positions.astype(F32)[:, None] * frequency[None, :]
    sign = jnp.where(lane < HEAD // 2, -1.0, 1.0).astype(F32)
    return jnp.cos(angles), jnp.sin(angles) * sign[None, :]


def exchange(x):
    return lax.all_to_all(x, "sp", split_axis=0, concat_axis=0, tiled=True)


def shards(projected, bias, cotangent, lengths, page_source):
    ways = lax.axis_size("sp")
    me = lax.axis_index("sp")
    rows = projected.shape[0]
    n = rows * ways
    page = page_source[0]
    recv0 = exchange(pack(0, ways, projected, cotangent))
    recv1 = exchange(pack(1, ways, projected, cotangent))

    ends = jnp.cumsum(lengths[0])
    starts = ends - lengths[0]
    tokens = jnp.arange(n, dtype=jnp.int32)
    first = jnp.max(jnp.where(tokens[:, None] >= starts[None, :], starts[None, :], 0), 1)
    first_block = first.reshape(n // BLK, BLK)[:, 0] // BLK
    cos, sin = rope_tables(tokens - first)
    first = first[None, :]

    qw = QUERY_HEADS * HEAD
    kw = KEY_VALUE_HEADS * HEAD
    kv_head = me // (ways // KEY_VALUE_HEADS)
    bias_rows = bias.reshape(-1, HEAD)
    qbias = lax.dynamic_slice_in_dim(bias_rows, me * 4, 4)
    kvbias = jnp.stack([bias_rows[QUERY_HEADS + kv_head], bias_rows[QUERY_HEADS + KEY_VALUE_HEADS + kv_head]])

    flat0 = recv0.reshape(n, 768)
    keys = make_keys(page, flat0, kvbias, cos, sin)
    none = jnp.zeros((8, HEAD), F32)
    send2, dk, dv, sums = attend(
        False, ways, first_block, page, flat0, keys, cos, sin, first, qbias[0:2], none, none, none
    )
    recv2 = exchange(send2)
    send3, _, _, sums = attend(
        True, ways, first_block, page, recv1.reshape(n, 512), keys, cos, sin, first, qbias[2:4], dk, dv, sums
    )
    sums = lax.psum(sums, "dp")
    recv3 = exchange(put_sums(sums, send3))
    att, gq = unpack0(recv2)
    att, gq, kvg, gb = unpack1(recv3, att, gq)
    return att, gq, kvg, gb.reshape(-1)


def solution(mesh):
    in_specs = (P(("dp", "sp"), None), P(), P(("dp", "sp"), None), P("dp", None), P("dp", None))
    out_specs = (P(("dp", "sp"), None), P(("dp", "sp"), None), P(("dp", "sp"), None), P())
    return jax.shard_map(shards, mesh=mesh, in_specs=in_specs, out_specs=out_specs, check_vma=False)
```

```python
import functools

import jax
import jax.numpy as jnp
from jax import lax
from jax.experimental import pallas as pl
from jax.experimental.pallas import tpu as pltpu
from jax.sharding import PartitionSpec as P

QUERY_HEADS = 64
KEY_VALUE_HEADS = 8
HEAD = 128
PAGE = 16
BLK = 256
SCALE = HEAD ** (-0.5)
LOG2E = 1.4426950408889634
NEG = -1e30
ROPE_BASE = 1000000.0

BF = jnp.bfloat16
F32 = jnp.float32
ANY = pl.BlockSpec(memory_space=pl.ANY)
VM = pl.BlockSpec(memory_space=pltpu.VMEM)
SM = pl.BlockSpec(memory_space=pltpu.SMEM)


def params(mib):
    return pltpu.CompilerParams(vmem_limit_bytes=mib * 1024 * 1024)


def cost(flops, nbytes):
    return pl.CostEstimate(flops=flops, bytes_accessed=nbytes, transcendentals=0)


def pack_kernel(chunk, ways, proj, cot, out, buf, sem, out_sem):
    kv0 = QUERY_HEADS * HEAD
    copies_of = ways // KEY_VALUE_HEADS
    fetch = []
    for d in range(ways):
        col = d * 512 + chunk * 256
        moves = [
            (proj.at[:, pl.ds(col, 256)], buf.at[d, :, pl.ds(0, 256)]),
            (cot.at[:, pl.ds(col, 256)], buf.at[d, :, pl.ds(256, 256)]),
        ]
        if chunk == 0:
            kcol = kv0 + (d // copies_of) * HEAD
            vcol = kcol + KEY_VALUE_HEADS * HEAD
            moves.append((proj.at[:, pl.ds(kcol, HEAD)], buf.at[d, :, pl.ds(512, HEAD)]))
            moves.append((proj.at[:, pl.ds(vcol, HEAD)], buf.at[d, :, pl.ds(640, HEAD)]))
        fetch.append([pltpu.make_async_copy(x, y, sem.at[d, m]) for m, (x, y) in enumerate(moves)])
    for group in fetch:
        for copy in group:
            copy.start()
    stores = []
    for d in range(ways):
        for copy in fetch[d]:
            copy.wait()
        stores.append(pltpu.make_async_copy(buf.at[d], out.at[d], out_sem.at[d]))
        stores[-1].start()
    for copy in stores:
        copy.wait()


def pack(chunk, ways, proj, cot):
    rows = proj.shape[0]
    width = 768 if chunk == 0 else 512
    return pl.pallas_call(
        functools.partial(pack_kernel, chunk, ways),
        out_shape=jax.ShapeDtypeStruct((ways, rows, width), BF),
        in_specs=[ANY, ANY],
        out_specs=ANY,
        scratch_shapes=[
            pltpu.VMEM((ways, rows, width), BF),
            pltpu.SemaphoreType.DMA((ways, 4)),
            pltpu.SemaphoreType.DMA((ways,)),
        ],
        compiler_params=params(8),
        cost_estimate=cost(0, 4 * ways * rows * width),
        name=f"pack{chunk}",
    )(proj, cot)


def rope(x, c, s):
    return x * c + pltpu.roll(x, HEAD // 2, 1) * s


def unrope(g, c, s):
    return g * c - pltpu.roll(g, HEAD // 2, 1) * s


def attend_kernel(last, *refs):
    if last:
        (first_block, page, recv, k, v, kt, vt, cos, sin, first, bias, dk_in, dv_in, sums_in,
         out, dk, dv, sums, q_raw, do_raw, st, ot, dqt, sem) = refs
    else:
        (first_block, page, recv, cos, sin, first, bias,
         out, k, v, kt, vt, dk, dv, sums, kv_raw, q_raw, do_raw, st, ot, dqt, sem) = refs
    n = recv.shape[0]
    blocks = n // BLK
    per = BLK // 128

    upstream = pltpu.make_async_copy(recv.at[:, pl.ds(256, 256)], do_raw, sem.at[0])
    upstream.start()

    def fetch(p, _):
        src = pl.ds(pl.multiple_of(page[p] * PAGE, PAGE), PAGE)
        dst = pl.ds(pl.multiple_of(p * PAGE, PAGE), PAGE)
        if not last:
            pltpu.make_async_copy(recv.at[src, pl.ds(512, 256)], kv_raw.at[dst, :], sem.at[2]).start()
        pltpu.make_async_copy(recv.at[src, pl.ds(0, 256)], q_raw.at[dst, :], sem.at[1]).start()
        return 0

    lax.fori_loop(0, n // PAGE, fetch, 0, unroll=4)
    if last:
        dk[...] = dk_in[...]
        dv[...] = dv_in[...]
    else:
        dk[...] = jnp.zeros_like(dk)
        dv[...] = jnp.zeros_like(dv)
        pltpu.make_async_copy(recv.at[:, pl.ds(512, 256)], kv_raw, sem.at[2]).wait()

        def prepare(b, _):
            rows = pl.ds(pl.multiple_of(b * BLK, BLK), BLK)
            x = rope(kv_raw[rows, 0:HEAD].astype(F32) + bias[2:3, :], cos[rows, :], sin[rows, :])
            y = kv_raw[rows, HEAD : 2 * HEAD].astype(F32) + bias[3:4, :]
            k[rows, :] = x.astype(BF)
            v[rows, :] = y.astype(BF)
            kt[:, rows] = jnp.transpose(x).astype(BF)
            vt[:, rows] = jnp.transpose(y).astype(BF)
            return 0

        lax.fori_loop(0, blocks, prepare, 0)
    pltpu.make_async_copy(recv.at[:, pl.ds(0, 256)], q_raw, sem.at[1]).wait()
    upstream.wait()

    nt = (((1,), (1,)), ((), ()))
    nn = (((1,), (0,)), ((), ()))

    def block(i, carry):
        rows = pl.ds(pl.multiple_of(i * BLK, BLK), BLK)
        c, s = cos[rows, :], sin[rows, :]
        q = jnp.concatenate(
            [
                rope(q_raw[rows, h * HEAD : (h + 1) * HEAD].astype(F32) + bias[h : h + 1, :], c, s).astype(BF)
                for h in range(2)
            ],
            0,
        )
        do = jnp.concatenate([do_raw[rows, 0:128], do_raw[rows, 128:256]], 0)
        lo = first_block[i]
        start1 = first[0:1, rows]
        start = jnp.concatenate([start1, start1], 1)
        lane = lax.broadcasted_iota(jnp.int32, (1, BLK), 1) + i * BLK
        token = jnp.concatenate([lane, lane], 1)

        def score(j, m):
            cols = pl.ds(pl.multiple_of(j * BLK, BLK), BLK)
            s = lax.dot_general(k[cols, :], q, nt, preferred_element_type=F32) * (SCALE * LOG2E)
            key = lax.broadcasted_iota(jnp.int32, (BLK, 2 * BLK), 0)
            s = jnp.where((key <= token - j * BLK) & (key >= start - j * BLK), s, NEG)
            st[j - lo] = s
            return jnp.maximum(m, jnp.max(s, 0, keepdims=True))

        m = lax.fori_loop(lo, i + 1, score, jnp.full((1, 2 * BLK), NEG, F32))
        ot[...] = jnp.zeros_like(ot)

        def value(j, total):
            cols = pl.ds(pl.multiple_of(j * BLK, BLK), BLK)
            e = jnp.exp2(st[j - lo] - m)
            st[j - lo] = e
            ot[...] += lax.dot_general(vt[:, cols], e.astype(BF), nn, preferred_element_type=F32)
            return total + jnp.sum(e, 0, keepdims=True)

        total = lax.fori_loop(lo, i + 1, value, jnp.zeros((1, 2 * BLK), F32))
        inv = 1.0 / total
        o_t = (ot[...] * inv).astype(BF).astype(F32)
        do_t = jnp.transpose(do.astype(F32))
        delta = jnp.sum(o_t * do_t, 0, keepdims=True)
        dqt[...] = jnp.zeros_like(dqt)

        def back(j, _):
            cols = pl.ds(pl.multiple_of(j * BLK, BLK), BLK)
            p = st[j - lo] * inv
            dp = lax.dot_general(v[cols, :], do, nt, preferred_element_type=F32)
            ds = (p * (dp - delta)).astype(BF)
            dv[cols, :] += lax.dot_general(p.astype(BF), do, nn, preferred_element_type=F32)
            dk[cols, :] += lax.dot_general(ds, q, nn, preferred_element_type=F32)
            dqt[...] += lax.dot_general(kt[:, cols], ds, nn, preferred_element_type=F32)
            return 0

        lax.fori_loop(lo, i + 1, back, 0)
        o = jnp.transpose(o_t).astype(BF)
        dq = jnp.transpose(dqt[...]) * SCALE
        new = []
        for h in range(2):
            g = unrope(dq[h * BLK : (h + 1) * BLK], c, s).astype(BF)
            new.append(carry[h] + jnp.sum(g.astype(F32), 0, keepdims=True))
            for a in range(per):
                part = slice(a * 128, (a + 1) * 128)
                out[i * per + a, :, h * HEAD : (h + 1) * HEAD] = o[h * BLK + a * 128 : h * BLK + (a + 1) * 128]
                out[i * per + a, :, 256 + h * HEAD : 256 + (h + 1) * HEAD] = g[part]
        return tuple(new)

    zero = jnp.zeros((1, HEAD), F32)
    head_sums = lax.fori_loop(0, blocks, block, (zero, zero))
    if not last:
        sums[...] = jnp.zeros_like(sums)
        sums[0:1, :] = head_sums[0]
        sums[1:2, :] = head_sums[1]
        return

    def finish(b, carry):
        rows = pl.ds(pl.multiple_of(b * 128, 128), 128)
        gk = unrope(dk[rows, :] * SCALE, cos[rows, :], sin[rows, :])
        gv = dv[rows, :]
        out[b, :, 512:640] = gk.astype(BF)
        out[b, :, 640:768] = gv.astype(BF)
        return (
            carry[0] + jnp.sum(gk, 0, keepdims=True),
            carry[1] + jnp.sum(gv, 0, keepdims=True),
        )

    kv_sums = lax.fori_loop(0, n // 128, finish, (zero, zero))
    sums[...] = sums_in[...]
    sums[2:3, :] = head_sums[0]
    sums[3:4, :] = head_sums[1]
    sums[4:5, :] = kv_sums[0]
    sums[5:6, :] = kv_sums[1]


def attend(last, ways, first_block, page, recv, cos, sin, first, bias, keys=(), state=()):
    n = recv.shape[0]
    grad = jax.ShapeDtypeStruct((n, HEAD), F32)
    row = jax.ShapeDtypeStruct((n, HEAD), BF)
    col = jax.ShapeDtypeStruct((HEAD, n), BF)
    sums = jax.ShapeDtypeStruct((8, HEAD), F32)
    out = jax.ShapeDtypeStruct((ways, n // ways, 768 if last else 512), BF)
    if last:
        args = (first_block, page, recv, *keys, cos, sin, first, bias, *state)
        outs = (out, sums)
        scratch = [pltpu.VMEM((n, HEAD), F32), pltpu.VMEM((n, HEAD), F32)]
    else:
        args = (first_block, page, recv, cos, sin, first, bias)
        outs = (out, row, row, col, col, grad, grad, sums)
        scratch = [pltpu.VMEM((n, 256), BF)]

    def body(*refs):
        if last:
            head, tail = refs[: len(args)], refs[len(args) :]
            o, sm, gk, gv = tail[:4]
            refs = (*head, o, gk, gv, sm, *tail[4:])
        attend_kernel(last, *refs)

    return pl.pallas_call(
        body,
        out_shape=outs,
        in_specs=[SM, SM, ANY] + [VM] * (len(args) - 3),
        out_specs=tuple([VM] * len(outs)),
        scratch_shapes=scratch
        + [
            pltpu.VMEM((n, 256), BF),
            pltpu.VMEM((n, 256), BF),
            pltpu.VMEM((1024 // BLK + 1, BLK, 2 * BLK), F32),
            pltpu.VMEM((HEAD, 2 * BLK), F32),
            pltpu.VMEM((HEAD, 2 * BLK), F32),
            pltpu.SemaphoreType.DMA((3,)),
        ],
        compiler_params=params(32),
        cost_estimate=cost(20 * 10**9, 10**7),
        name="attend1" if last else "attend0",
    )(*args)


def unpack_heads(recv, buf, att, gq, chunk, sem, out_sem):
    ways = buf.shape[0]
    fetch = [pltpu.make_async_copy(recv.at[d], buf.at[d], sem.at[d]) for d in range(ways)]
    for copy in fetch:
        copy.start()
    stores = []
    for d in range(ways):
        cols = pl.ds(d * 512 + chunk * 256, 256)
        fetch[d].wait()
        stores.append(pltpu.make_async_copy(buf.at[d, :, pl.ds(0, 256)], att.at[:, cols], out_sem.at[d, 0]))
        stores.append(pltpu.make_async_copy(buf.at[d, :, pl.ds(256, 256)], gq.at[:, cols], out_sem.at[d, 1]))
        stores[-2].start()
        stores[-1].start()
    return stores


def unpack0_kernel(recv, att, gq, buf, sem, out_sem):
    for copy in unpack_heads(recv, buf, att, gq, 0, sem, out_sem):
        copy.wait()


def unpack_scratch(recv):
    ways = recv.shape[0]
    return [
        pltpu.VMEM(recv.shape, BF),
        pltpu.SemaphoreType.DMA((ways,)),
        pltpu.SemaphoreType.DMA((ways, 2)),
    ]


def unpack0(recv):
    ways, rows, _ = recv.shape
    shape = jax.ShapeDtypeStruct((rows, QUERY_HEADS * HEAD), BF)
    return pl.pallas_call(
        unpack0_kernel,
        out_shape=(shape, shape),
        in_specs=[ANY],
        out_specs=(ANY, ANY),
        scratch_shapes=unpack_scratch(recv),
        compiler_params=params(8),
        cost_estimate=cost(0, 4 * ways * rows * 512),
        name="unpack0",
    )(recv)


def unpack1_kernel(recv, _a, _g, att, gq, kvg, buf, sem, out_sem):
    ways = buf.shape[0]
    stores = unpack_heads(recv, buf, att, gq, 1, sem, out_sem)
    share = ways // KEY_VALUE_HEADS
    kw = KEY_VALUE_HEADS * HEAD
    for h in range(KEY_VALUE_HEADS):
        grad = buf[h * share, :, 512:768].astype(F32)
        for r in range(1, share):
            grad = grad + buf[h * share + r, :, 512:768].astype(F32)
        kvg[:, h * HEAD : (h + 1) * HEAD] = grad[:, :HEAD].astype(BF)
        kvg[:, kw + h * HEAD : kw + (h + 1) * HEAD] = grad[:, HEAD:].astype(BF)
    for copy in stores:
        copy.wait()


def unpack1(recv, att, gq):
    ways = recv.shape[0]
    rows = att.shape[0]
    return pl.pallas_call(
        unpack1_kernel,
        out_shape=(
            jax.ShapeDtypeStruct(att.shape, BF),
            jax.ShapeDtypeStruct(gq.shape, BF),
            jax.ShapeDtypeStruct((rows, 2 * KEY_VALUE_HEADS * HEAD), BF),
        ),
        in_specs=[ANY, ANY, ANY],
        out_specs=(ANY, ANY, VM),
        input_output_aliases={1: 0, 2: 1},
        scratch_shapes=unpack_scratch(recv),
        compiler_params=params(8),
        cost_estimate=cost(0, 4 * ways * rows * 768),
        name="unpack1",
    )(recv, att, gq)


def rope_tables(positions):
    lane = jnp.arange(HEAD, dtype=jnp.int32)
    exponent = (lane % (HEAD // 2)).astype(F32) * 2.0 / HEAD
    frequency = jnp.power(jnp.float32(ROPE_BASE), -exponent)
    angles = positions.astype(F32)[:, None] * frequency[None, :]
    sign = jnp.where(lane < HEAD // 2, -1.0, 1.0).astype(F32)
    return jnp.cos(angles), jnp.sin(angles) * sign[None, :]


def exchange(x):
    return lax.all_to_all(x, "sp", split_axis=0, concat_axis=0, tiled=True)


def shards(projected, bias, cotangent, lengths, page_source):
    ways = lax.axis_size("sp")
    me = lax.axis_index("sp")
    rows = projected.shape[0]
    n = rows * ways
    page = page_source[0]
    recv0 = exchange(pack(0, ways, projected, cotangent))
    recv1 = exchange(pack(1, ways, projected, cotangent))

    ends = jnp.cumsum(lengths[0])
    starts = ends - lengths[0]
    tokens = jnp.arange(n, dtype=jnp.int32)
    first = jnp.max(jnp.where(tokens[:, None] >= starts[None, :], starts[None, :], 0), 1)
    first_block = first.reshape(n // BLK, BLK)[:, 0] // BLK
    cos, sin = rope_tables(tokens - first)
    first = first[None, :]

    share = ways // KEY_VALUE_HEADS
    kv_head = me // share
    bias_rows = bias.reshape(-1, HEAD)
    qbias = lax.dynamic_slice_in_dim(bias_rows, me * 4, 4)
    kbias = lax.dynamic_slice_in_dim(bias_rows, QUERY_HEADS + kv_head, 1)
    vbias = lax.dynamic_slice_in_dim(bias_rows, QUERY_HEADS + KEY_VALUE_HEADS + kv_head, 1)
    bias0 = jnp.concatenate([qbias[0:2], kbias, vbias], 0)

    send2, k, v, kt, vt, dk, dv, sums = attend(
        False, ways, first_block, page, recv0.reshape(n, 768), cos, sin, first, bias0
    )
    recv2 = exchange(send2)
    send3, sums = attend(
        True, ways, first_block, page, recv1.reshape(n, 512), cos, sin, first, qbias[2:4],
        (k, v, kt, vt), (dk, dv, sums),
    )
    recv3 = exchange(send3)
    sums = lax.all_gather(lax.psum(sums, "dp"), "sp")
    att, gq = unpack0(recv2)
    att, gq, kvg = unpack1(recv3, att, gq)
    kv_sums = jnp.sum(sums[:, 4:6].reshape(KEY_VALUE_HEADS, share, 2, HEAD), 1)
    gb = jnp.concatenate(
        [sums[:, 0:4].reshape(-1), kv_sums[:, 0].reshape(-1), kv_sums[:, 1].reshape(-1)]
    )
    return att, gq, kvg, gb


def solution(mesh):
    in_specs = (P(("dp", "sp"), None), P(), P(("dp", "sp"), None), P("dp", None), P("dp", None))
    out_specs = (P(("dp", "sp"), None), P(("dp", "sp"), None), P(("dp", "sp"), None), P())
    return jax.shard_map(shards, mesh=mesh, in_specs=in_specs, out_specs=out_specs, check_vma=False)
```

```python
import functools

import jax
import jax.numpy as jnp
from jax import lax
from jax.experimental import pallas as pl
from jax.experimental.pallas import tpu as pltpu
from jax.sharding import PartitionSpec as P

QUERY_HEADS = 64
KEY_VALUE_HEADS = 8
HEAD = 128
PAGE = 16
BLK = 256
SCALE = HEAD ** (-0.5)
LOG2E = 1.4426950408889634
NEG = -1e30
ROPE_BASE = 1000000.0
EXTRA = 8

BF = jnp.bfloat16
F32 = jnp.float32
ANY = pl.BlockSpec(memory_space=pl.ANY)
HBM = pl.BlockSpec(memory_space=pltpu.HBM)
VM = pl.BlockSpec(memory_space=pltpu.VMEM)
SM = pl.BlockSpec(memory_space=pltpu.SMEM)


def params(mib):
    return pltpu.CompilerParams(vmem_limit_bytes=mib * 1024 * 1024)


def cost(flops, nbytes):
    return pl.CostEstimate(flops=flops, bytes_accessed=nbytes, transcendentals=0)


def run_copies(copies):
    for copy in copies:
        copy.start()
    for copy in copies:
        copy.wait()


def pack_kernel(chunk, ways, proj, cot, out, buf, sem, out_sem):
    kv0 = QUERY_HEADS * HEAD
    copies_of = ways // KEY_VALUE_HEADS
    fetch = []
    for d in range(ways):
        col = d * 512 + chunk * 256
        moves = [
            (proj.at[:, pl.ds(col, 256)], buf.at[d, :, pl.ds(0, 256)]),
            (cot.at[:, pl.ds(col, 256)], buf.at[d, :, pl.ds(256, 256)]),
        ]
        if chunk == 0:
            kcol = kv0 + (d // copies_of) * HEAD
            vcol = kcol + KEY_VALUE_HEADS * HEAD
            moves.append((proj.at[:, pl.ds(kcol, HEAD)], buf.at[d, :, pl.ds(512, HEAD)]))
            moves.append((proj.at[:, pl.ds(vcol, HEAD)], buf.at[d, :, pl.ds(640, HEAD)]))
        fetch.append([pltpu.make_async_copy(x, y, sem.at[d, m]) for m, (x, y) in enumerate(moves)])
    for group in fetch:
        for copy in group:
            copy.start()
    stores = []
    for d in range(ways):
        for copy in fetch[d]:
            copy.wait()
        stores.append(pltpu.make_async_copy(buf.at[d], out.at[d], out_sem.at[d]))
        stores[-1].start()
    for copy in stores:
        copy.wait()


def pack(chunk, ways, proj, cot):
    rows = proj.shape[0]
    width = 768 if chunk == 0 else 512
    return pl.pallas_call(
        functools.partial(pack_kernel, chunk, ways),
        out_shape=jax.ShapeDtypeStruct((ways, rows, width), BF),
        in_specs=[ANY, ANY],
        out_specs=ANY,
        scratch_shapes=[
            pltpu.VMEM((ways, rows, width), BF),
            pltpu.SemaphoreType.DMA((ways, 4)),
            pltpu.SemaphoreType.DMA((ways,)),
        ],
        compiler_params=params(60),
        cost_estimate=cost(0, 4 * ways * rows * width),
        name=f"pack{chunk}",
    )(proj, cot)


def rope(x, c, s):
    return x * c + pltpu.roll(x, HEAD // 2, 1) * s


def unrope(g, c, s):
    return g * c - pltpu.roll(g, HEAD // 2, 1) * s


def attend_kernel(last, *refs):
    if last:
        (first_block, page, recv, k, v, kt, vt, cos, sin, first, bias, dk_in, dv_in, sums_in,
         out, dk, dv, sums, q_raw, do_raw, st, ot, dqt, sem) = refs
    else:
        (first_block, page, recv, cos, sin, first, bias,
         out, k, v, kt, vt, dk, dv, sums, kv_raw, q_raw, do_raw, st, ot, dqt, sem) = refs
    n = recv.shape[0]
    blocks = n // BLK
    per = BLK // 128

    upstream = pltpu.make_async_copy(recv.at[:, pl.ds(256, 256)], do_raw, sem.at[0])
    upstream.start()

    def fetch(p, _):
        src = pl.ds(pl.multiple_of(page[p] * PAGE, PAGE), PAGE)
        dst = pl.ds(pl.multiple_of(p * PAGE, PAGE), PAGE)
        if not last:
            pltpu.make_async_copy(recv.at[src, pl.ds(512, 256)], kv_raw.at[dst, :], sem.at[2]).start()
        pltpu.make_async_copy(recv.at[src, pl.ds(0, 256)], q_raw.at[dst, :], sem.at[1]).start()
        return 0

    lax.fori_loop(0, n // PAGE, fetch, 0, unroll=4)
    if last:
        dk[...] = dk_in[...]
        dv[...] = dv_in[...]
    else:
        dk[...] = jnp.zeros_like(dk)
        dv[...] = jnp.zeros_like(dv)
        pltpu.make_async_copy(recv.at[:, pl.ds(512, 256)], kv_raw, sem.at[2]).wait()

        def prepare(b, _):
            rows = pl.ds(pl.multiple_of(b * BLK, BLK), BLK)
            x = rope(kv_raw[rows, 0:HEAD].astype(F32) + bias[2:3, :], cos[rows, :], sin[rows, :])
            y = kv_raw[rows, HEAD : 2 * HEAD].astype(F32) + bias[3:4, :]
            k[rows, :] = x.astype(BF)
            v[rows, :] = y.astype(BF)
            kt[:, rows] = jnp.transpose(x).astype(BF)
            vt[:, rows] = jnp.transpose(y).astype(BF)
            return 0

        lax.fori_loop(0, blocks, prepare, 0)
    pltpu.make_async_copy(recv.at[:, pl.ds(0, 256)], q_raw, sem.at[1]).wait()
    upstream.wait()

    nt = (((1,), (1,)), ((), ()))
    nn = (((1,), (0,)), ((), ()))

    def block(i, carry):
        rows = pl.ds(pl.multiple_of(i * BLK, BLK), BLK)
        c, s = cos[rows, :], sin[rows, :]
        q = jnp.concatenate(
            [
                rope(q_raw[rows, h * HEAD : (h + 1) * HEAD].astype(F32) + bias[h : h + 1, :], c, s).astype(BF)
                for h in range(2)
            ],
            0,
        )
        do = jnp.concatenate([do_raw[rows, 0:128], do_raw[rows, 128:256]], 0)
        lo = first_block[i]
        start1 = first[0:1, rows]
        start = jnp.concatenate([start1, start1], 1)
        lane = lax.broadcasted_iota(jnp.int32, (1, BLK), 1) + i * BLK
        token = jnp.concatenate([lane, lane], 1)

        def score(j, m):
            cols = pl.ds(pl.multiple_of(j * BLK, BLK), BLK)
            s = lax.dot_general(k[cols, :], q, nt, preferred_element_type=F32) * (SCALE * LOG2E)
            key = lax.broadcasted_iota(jnp.int32, (BLK, 2 * BLK), 0)
            s = jnp.where((key <= token - j * BLK) & (key >= start - j * BLK), s, NEG)
            st[j - lo] = s
            return jnp.maximum(m, jnp.max(s, 0, keepdims=True))

        m = lax.fori_loop(lo, i + 1, score, jnp.full((1, 2 * BLK), NEG, F32))
        ot[...] = jnp.zeros_like(ot)

        def value(j, total):
            cols = pl.ds(pl.multiple_of(j * BLK, BLK), BLK)
            e = jnp.exp2(st[j - lo] - m)
            st[j - lo] = e
            ot[...] += lax.dot_general(vt[:, cols], e.astype(BF), nn, preferred_element_type=F32)
            return total + jnp.sum(e, 0, keepdims=True)

        total = lax.fori_loop(lo, i + 1, value, jnp.zeros((1, 2 * BLK), F32))
        inv = 1.0 / total
        o_t = (ot[...] * inv).astype(BF).astype(F32)
        do_t = jnp.transpose(do.astype(F32))
        delta = jnp.sum(o_t * do_t, 0, keepdims=True)
        dqt[...] = jnp.zeros_like(dqt)

        def back(j, _):
            cols = pl.ds(pl.multiple_of(j * BLK, BLK), BLK)
            p = st[j - lo] * inv
            dp = lax.dot_general(v[cols, :], do, nt, preferred_element_type=F32)
            ds = (p * (dp - delta)).astype(BF)
            dv[cols, :] += lax.dot_general(p.astype(BF), do, nn, preferred_element_type=F32)
            dk[cols, :] += lax.dot_general(ds, q, nn, preferred_element_type=F32)
            dqt[...] += lax.dot_general(kt[:, cols], ds, nn, preferred_element_type=F32)
            return 0

        lax.fori_loop(lo, i + 1, back, 0)
        o = jnp.transpose(o_t).astype(BF)
        dq = jnp.transpose(dqt[...]) * SCALE
        new = []
        for h in range(2):
            g = unrope(dq[h * BLK : (h + 1) * BLK], c, s).astype(BF)
            new.append(carry[h] + jnp.sum(g.astype(F32), 0, keepdims=True))
            for a in range(per):
                part = slice(a * 128, (a + 1) * 128)
                out[i * per + a, 0:128, h * HEAD : (h + 1) * HEAD] = o[h * BLK + a * 128 : h * BLK + (a + 1) * 128]
                out[i * per + a, 0:128, 256 + h * HEAD : 256 + (h + 1) * HEAD] = g[part]
        return tuple(new)

    zero = jnp.zeros((1, HEAD), F32)
    head_sums = lax.fori_loop(0, blocks, block, (zero, zero))
    if not last:
        sums[...] = jnp.zeros_like(sums)
        sums[0:1, :] = head_sums[0]
        sums[1:2, :] = head_sums[1]
        return

    def finish(b, carry):
        rows = pl.ds(pl.multiple_of(b * 128, 128), 128)
        gk = unrope(dk[rows, :] * SCALE, cos[rows, :], sin[rows, :])
        gv = dv[rows, :]
        out[b, 0:128, 512:640] = gk.astype(BF)
        out[b, 0:128, 640:768] = gv.astype(BF)
        return (
            carry[0] + jnp.sum(gk, 0, keepdims=True),
            carry[1] + jnp.sum(gv, 0, keepdims=True),
        )

    kv_sums = lax.fori_loop(0, n // 128, finish, (zero, zero))
    sums[...] = sums_in[...]
    sums[2:3, :] = head_sums[0]
    sums[3:4, :] = head_sums[1]
    sums[4:5, :] = kv_sums[0]
    sums[5:6, :] = kv_sums[1]


def attend(last, ways, first_block, page, recv, cos, sin, first, bias, keys=(), state=()):
    n = recv.shape[0]
    grad = jax.ShapeDtypeStruct((n, HEAD), F32)
    row = jax.ShapeDtypeStruct((n, HEAD), BF)
    col = jax.ShapeDtypeStruct((HEAD, n), BF)
    sums = jax.ShapeDtypeStruct((8, HEAD), F32)
    out = jax.ShapeDtypeStruct((ways, n // ways + (EXTRA if last else 0), 768 if last else 512), BF)
    if last:
        args = (first_block, page, recv, *keys, cos, sin, first, bias, *state)
        outs = (out, sums)
        scratch = [pltpu.VMEM((n, HEAD), F32), pltpu.VMEM((n, HEAD), F32)]
    else:
        args = (first_block, page, recv, cos, sin, first, bias)
        outs = (out, row, row, col, col, grad, grad, sums)
        scratch = [pltpu.VMEM((n, 256), BF)]

    def body(*refs):
        if last:
            head, tail = refs[: len(args)], refs[len(args) :]
            o, sm, gk, gv = tail[:4]
            refs = (*head, o, gk, gv, sm, *tail[4:])
        attend_kernel(last, *refs)

    return pl.pallas_call(
        body,
        out_shape=outs,
        in_specs=[SM, SM, HBM] + [VM] * (len(args) - 3),
        out_specs=tuple([VM] * len(outs)),
        scratch_shapes=scratch
        + [
            pltpu.VMEM((n, 256), BF),
            pltpu.VMEM((n, 256), BF),
            pltpu.VMEM((1024 // BLK + 1, BLK, 2 * BLK), F32),
            pltpu.VMEM((HEAD, 2 * BLK), F32),
            pltpu.VMEM((HEAD, 2 * BLK), F32),
            pltpu.SemaphoreType.DMA((3,)),
        ],
        compiler_params=params(60),
        cost_estimate=cost(20 * 10**9, 10**7),
        name="attend1" if last else "attend0",
    )(*args)


def sums_kernel(sums, _, out, rows, sem):
    for r in range(6):
        x = sums[r : r + 1, :]
        hi = x.astype(BF).astype(F32)
        mid = (x - hi).astype(BF).astype(F32)
        low = x - hi - mid
        rows[:, r * HEAD : (r + 1) * HEAD] = jnp.concatenate(
            [hi, mid, low, jnp.zeros((EXTRA - 3, HEAD), F32)], 0
        ).astype(BF)
    run_copies(
        [
            pltpu.make_async_copy(rows, out.at[d, pl.ds(128, EXTRA), :], sem.at[d])
            for d in range(out.shape[0])
        ]
    )


def put_sums(sums, payload):
    ways = payload.shape[0]
    return pl.pallas_call(
        sums_kernel,
        out_shape=jax.ShapeDtypeStruct(payload.shape, payload.dtype),
        in_specs=[VM, ANY],
        out_specs=ANY,
        input_output_aliases={1: 0},
        scratch_shapes=[pltpu.VMEM((EXTRA, 768), BF), pltpu.SemaphoreType.DMA((ways,))],
        compiler_params=params(60),
        name="sums",
    )(sums, payload)


def head_copies(recv, att, gq, chunk, sem):
    copies = []
    for d in range(recv.shape[0]):
        cols = pl.ds(d * 512 + chunk * 256, 256)
        rows = pl.ds(0, 128)
        copies.append(pltpu.make_async_copy(recv.at[d, rows, pl.ds(0, 256)], att.at[:, cols], sem.at[d, 0]))
        copies.append(pltpu.make_async_copy(recv.at[d, rows, pl.ds(256, 256)], gq.at[:, cols], sem.at[d, 1]))
    return copies


def unpack0_kernel(recv, att, gq, sem):
    run_copies(head_copies(recv, att, gq, 0, sem))


def unpack0(recv):
    ways, rows, _ = recv.shape
    shape = jax.ShapeDtypeStruct((rows, QUERY_HEADS * HEAD), BF)
    return pl.pallas_call(
        unpack0_kernel,
        out_shape=(shape, shape),
        in_specs=[VM],
        out_specs=(ANY, ANY),
        scratch_shapes=[pltpu.SemaphoreType.DMA((ways, 2))],
        compiler_params=params(60),
        cost_estimate=cost(0, 4 * ways * rows * 512),
        name="unpack0",
    )(recv)


def unpack1_kernel(recv, _a, _g, att, gq, kvg, gb, sem):
    ways = recv.shape[0]
    copies = head_copies(recv, att, gq, 1, sem)
    for copy in copies:
        copy.start()
    share = ways // KEY_VALUE_HEADS
    qw = QUERY_HEADS * HEAD
    kw = KEY_VALUE_HEADS * HEAD

    def sums_of(d):
        t = recv[d, 128 : 128 + EXTRA, :].astype(F32)
        return t[0:1] + t[1:2] + t[2:3]

    for h in range(KEY_VALUE_HEADS):
        grad = jnp.zeros((128, 256), F32)
        kvsum = jnp.zeros((1, 256), F32)
        for r in range(share):
            d = h * share + r
            grad = grad + recv[d, 0:128, 512:768].astype(F32)
            b = sums_of(d)
            gb[:, d * 512 : (d + 1) * 512] = b[:, 0:512]
            kvsum = kvsum + b[:, 512:768]
        kvg[:, h * HEAD : (h + 1) * HEAD] = grad[:, :HEAD].astype(BF)
        kvg[:, kw + h * HEAD : kw + (h + 1) * HEAD] = grad[:, HEAD:].astype(BF)
        gb[:, qw + h * HEAD : qw + (h + 1) * HEAD] = kvsum[:, :HEAD]
        gb[:, qw + kw + h * HEAD : qw + kw + (h + 1) * HEAD] = kvsum[:, HEAD:]
    for copy in copies:
        copy.wait()


def unpack1(recv, att, gq):
    ways = recv.shape[0]
    rows = att.shape[0]
    return pl.pallas_call(
        unpack1_kernel,
        out_shape=(
            jax.ShapeDtypeStruct(att.shape, BF),
            jax.ShapeDtypeStruct(gq.shape, BF),
            jax.ShapeDtypeStruct((rows, 2 * KEY_VALUE_HEADS * HEAD), BF),
            jax.ShapeDtypeStruct((1, (QUERY_HEADS + 2 * KEY_VALUE_HEADS) * HEAD), F32),
        ),
        in_specs=[VM, HBM, HBM],
        out_specs=(HBM, HBM, VM, VM),
        input_output_aliases={1: 0, 2: 1},
        scratch_shapes=[pltpu.SemaphoreType.DMA((ways, 2))],
        compiler_params=params(8),
        cost_estimate=cost(0, 4 * ways * rows * 768),
        name="unpack1",
    )(recv, att, gq)


def rope_tables(positions):
    lane = jnp.arange(HEAD, dtype=jnp.int32)
    exponent = (lane % (HEAD // 2)).astype(F32) * 2.0 / HEAD
    frequency = jnp.power(jnp.float32(ROPE_BASE), -exponent)
    angles = positions.astype(F32)[:, None] * frequency[None, :]
    sign = jnp.where(lane < HEAD // 2, -1.0, 1.0).astype(F32)
    return jnp.cos(angles), jnp.sin(angles) * sign[None, :]


def exchange(x):
    return lax.all_to_all(x, "sp", split_axis=0, concat_axis=0, tiled=True)


def shards(projected, bias, cotangent, lengths, page_source):
    ways = lax.axis_size("sp")
    me = lax.axis_index("sp")
    rows = projected.shape[0]
    n = rows * ways
    page = page_source[0]
    recv0 = exchange(pack(0, ways, projected, cotangent))
    recv1 = exchange(pack(1, ways, projected, cotangent))

    ends = jnp.cumsum(lengths[0])
    starts = ends - lengths[0]
    tokens = jnp.arange(n, dtype=jnp.int32)
    first = jnp.max(jnp.where(tokens[:, None] >= starts[None, :], starts[None, :], 0), 1)
    first_block = first.reshape(n // BLK, BLK)[:, 0] // BLK
    cos, sin = rope_tables(tokens - first)
    first = first[None, :]

    share = ways // KEY_VALUE_HEADS
    kv_head = me // share
    bias_rows = bias.reshape(-1, HEAD)
    qbias = lax.dynamic_slice_in_dim(bias_rows, me * 4, 4)
    kbias = lax.dynamic_slice_in_dim(bias_rows, QUERY_HEADS + kv_head, 1)
    vbias = lax.dynamic_slice_in_dim(bias_rows, QUERY_HEADS + KEY_VALUE_HEADS + kv_head, 1)
    bias0 = jnp.concatenate([qbias[0:2], kbias, vbias], 0)

    send2, k, v, kt, vt, dk, dv, sums = attend(
        False, ways, first_block, page, recv0.reshape(n, 768), cos, sin, first, bias0
    )
    recv2 = exchange(send2)
    send3, sums = attend(
        True, ways, first_block, page, recv1.reshape(n, 512), cos, sin, first, qbias[2:4],
        (k, v, kt, vt), (dk, dv, sums),
    )
    recv3 = exchange(put_sums(lax.psum(sums, "dp"), send3))
    att, gq = unpack0(recv2)
    att, gq, kvg, gb = unpack1(recv3, att, gq)
    return att, gq, kvg, gb.reshape(-1)


def solution(mesh):
    in_specs = (P(("dp", "sp"), None), P(), P(("dp", "sp"), None), P("dp", None), P("dp", None))
    out_specs = (P(("dp", "sp"), None), P(("dp", "sp"), None), P(("dp", "sp"), None), P())
    return jax.shard_map(shards, mesh=mesh, in_specs=in_specs, out_specs=out_specs, check_vma=False)
```

```python
import functools

import jax
import jax.numpy as jnp
from jax import lax
from jax.experimental import pallas as pl
from jax.experimental.pallas import tpu as pltpu
from jax.sharding import PartitionSpec as P

QUERY_HEADS = 64
KEY_VALUE_HEADS = 8
HEAD = 128
PAGE = 16
BLK = 256
SCALE = HEAD ** (-0.5)
LOG2E = 1.4426950408889634
NEG = -1e30
ROPE_BASE = 1000000.0
SIDE = 4

BF = jnp.bfloat16
F32 = jnp.float32
ANY = pl.BlockSpec(memory_space=pl.ANY)
HBM = pl.BlockSpec(memory_space=pltpu.HBM)
VM = pl.BlockSpec(memory_space=pltpu.VMEM)
SM = pl.BlockSpec(memory_space=pltpu.SMEM)


def params(mib):
    return pltpu.CompilerParams(vmem_limit_bytes=mib * 1024 * 1024)


def cost(flops, nbytes):
    return pl.CostEstimate(flops=flops, bytes_accessed=nbytes, transcendentals=0)


def run_copies(copies):
    for copy in copies:
        copy.start()
    for copy in copies:
        copy.wait()


def pack_kernel(chunk, ways, proj, cot, out, buf, sem, out_sem):
    kv0 = QUERY_HEADS * HEAD
    copies_of = ways // KEY_VALUE_HEADS
    fetch = []
    for d in range(ways):
        col = d * 512 + chunk * 256
        moves = [
            (proj.at[:, pl.ds(col, 256)], buf.at[d, :, pl.ds(0, 256)]),
            (cot.at[:, pl.ds(col, 256)], buf.at[d, :, pl.ds(256, 256)]),
        ]
        if chunk == 0:
            kcol = kv0 + (d // copies_of) * HEAD
            vcol = kcol + KEY_VALUE_HEADS * HEAD
            moves.append((proj.at[:, pl.ds(kcol, HEAD)], buf.at[d, :, pl.ds(512, HEAD)]))
            moves.append((proj.at[:, pl.ds(vcol, HEAD)], buf.at[d, :, pl.ds(640, HEAD)]))
        fetch.append([pltpu.make_async_copy(x, y, sem.at[d, m]) for m, (x, y) in enumerate(moves)])
    for group in fetch:
        for copy in group:
            copy.start()
    stores = []
    for d in range(ways):
        for copy in fetch[d]:
            copy.wait()
        stores.append(pltpu.make_async_copy(buf.at[d], out.at[d], out_sem.at[d]))
        stores[-1].start()
    for copy in stores:
        copy.wait()


def pack(chunk, ways, proj, cot):
    rows = proj.shape[0]
    width = 768 if chunk == 0 else 512
    return pl.pallas_call(
        functools.partial(pack_kernel, chunk, ways),
        out_shape=jax.ShapeDtypeStruct((ways, rows, width), BF),
        in_specs=[ANY, ANY],
        out_specs=ANY,
        scratch_shapes=[
            pltpu.VMEM((ways, rows, width), BF),
            pltpu.SemaphoreType.DMA((ways, 4)),
            pltpu.SemaphoreType.DMA((ways,)),
        ],
        compiler_params=params(60),
        cost_estimate=cost(0, 4 * ways * rows * width),
        name=f"pack{chunk}",
    )(proj, cot)


def rope(x, c, s):
    return x * c + pltpu.roll(x, HEAD // 2, 1) * s


def unrope(g, c, s):
    return g * c - pltpu.roll(g, HEAD // 2, 1) * s


def attend_kernel(last, *refs):
    if last:
        (first_block, page, recv, k_in, v_in, kt_in, vt_in, cos_in, sin_in, dk_in, dv_in, first, bias, sums_in,
         out_hbm, sums,
         k, v, kt, vt, cos, sin, dk, dv, dk_old, dv_old, q_raw, do_raw, st, ot, dqt, out,
         sem, key_sem, grad_sem, out_sem) = refs
        loads = [(k_in, k), (v_in, v), (kt_in, kt), (vt_in, vt)]
    else:
        (first_block, page, recv, cos_in, sin_in, first, bias,
         out_hbm, k_out, v_out, kt_out, vt_out, dk, dv, sums,
         k, v, kt, vt, cos, sin, kv_raw, q_raw, do_raw, st, ot, dqt, out,
         sem, key_sem, out_sem) = refs
        loads = []
    n = recv.shape[0]
    blocks = n // BLK
    per = BLK // 128

    upstream = pltpu.make_async_copy(recv.at[:, pl.ds(256, 256)], do_raw, sem.at[0])
    tables = [
        pltpu.make_async_copy(cos_in, cos, sem.at[3]),
        pltpu.make_async_copy(sin_in, sin, sem.at[4]),
    ]
    keys = [pltpu.make_async_copy(x, y, key_sem.at[m]) for m, (x, y) in enumerate(loads)]

    def fetch(p, _):
        src = pl.ds(pl.multiple_of(page[p] * PAGE, PAGE), PAGE)
        dst = pl.ds(pl.multiple_of(p * PAGE, PAGE), PAGE)
        if not last:
            pltpu.make_async_copy(recv.at[src, pl.ds(512, 256)], kv_raw.at[dst, :], sem.at[2]).start()
        pltpu.make_async_copy(recv.at[src, pl.ds(0, 256)], q_raw.at[dst, :], sem.at[1]).start()
        return 0

    for copy in tables:
        copy.start()
    lax.fori_loop(0, n // PAGE, fetch, 0, unroll=4)
    for copy in keys + [upstream]:
        copy.start()
    dk[...] = jnp.zeros_like(dk)
    dv[...] = jnp.zeros_like(dv)
    for copy in tables:
        copy.wait()
    if last:
        old = [
            pltpu.make_async_copy(dk_in, dk_old, grad_sem.at[0]),
            pltpu.make_async_copy(dv_in, dv_old, grad_sem.at[1]),
        ]
        for copy in old:
            copy.start()
        for copy in keys:
            copy.wait()
    else:
        pltpu.make_async_copy(recv.at[:, pl.ds(512, 256)], kv_raw, sem.at[2]).wait()

        def prepare(b, _):
            rows = pl.ds(pl.multiple_of(b * BLK, BLK), BLK)
            x = rope(kv_raw[rows, 0:HEAD].astype(F32) + bias[2:3, :], cos[rows, :], sin[rows, :])
            y = kv_raw[rows, HEAD : 2 * HEAD].astype(F32) + bias[3:4, :]
            k[rows, :] = x.astype(BF)
            v[rows, :] = y.astype(BF)
            kt[:, rows] = jnp.transpose(x).astype(BF)
            vt[:, rows] = jnp.transpose(y).astype(BF)
            return 0

        lax.fori_loop(0, blocks, prepare, 0)
        saves = [
            pltpu.make_async_copy(x, y, key_sem.at[m])
            for m, (x, y) in enumerate([(k, k_out), (v, v_out), (kt, kt_out), (vt, vt_out)])
        ]
        for copy in saves:
            copy.start()
    pltpu.make_async_copy(recv.at[:, pl.ds(0, 256)], q_raw, sem.at[1]).wait()
    upstream.wait()

    def heads_out(d):
        return pltpu.make_async_copy(
            out.at[d, :, pl.ds(0, 512)], out_hbm.at[d, :, pl.ds(0, 512)], out_sem.at[d, 0]
        )

    def pair_out(d):
        return pltpu.make_async_copy(
            out.at[d, :, pl.ds(512, 256)], out_hbm.at[d, :, pl.ds(512, 256)], out_sem.at[d, 1]
        )

    nt = (((1,), (1,)), ((), ()))
    nn = (((1,), (0,)), ((), ()))

    def block(i, carry):
        rows = pl.ds(pl.multiple_of(i * BLK, BLK), BLK)
        c, s = cos[rows, :], sin[rows, :]
        q = jnp.concatenate(
            [
                rope(q_raw[rows, h * HEAD : (h + 1) * HEAD].astype(F32) + bias[h : h + 1, :], c, s).astype(BF)
                for h in range(2)
            ],
            0,
        )
        do = jnp.concatenate([do_raw[rows, 0:128], do_raw[rows, 128:256]], 0)
        lo = first_block[i]
        start1 = first[0:1, rows]
        start = jnp.concatenate([start1, start1], 1)
        lane = lax.broadcasted_iota(jnp.int32, (1, BLK), 1) + i * BLK
        token = jnp.concatenate([lane, lane], 1)

        def score(j, m):
            cols = pl.ds(pl.multiple_of(j * BLK, BLK), BLK)
            s = lax.dot_general(k[cols, :], q, nt, preferred_element_type=F32) * (SCALE * LOG2E)
            key = lax.broadcasted_iota(jnp.int32, (BLK, 2 * BLK), 0)
            s = jnp.where((key <= token - j * BLK) & (key >= start - j * BLK), s, NEG)
            st[j - lo] = s
            return jnp.maximum(m, jnp.max(s, 0, keepdims=True))

        m = lax.fori_loop(lo, i + 1, score, jnp.full((1, 2 * BLK), NEG, F32))
        ot[...] = jnp.zeros_like(ot)

        def value(j, total):
            cols = pl.ds(pl.multiple_of(j * BLK, BLK), BLK)
            e = jnp.exp2(st[j - lo] - m)
            st[j - lo] = e
            ot[...] += lax.dot_general(vt[:, cols], e.astype(BF), nn, preferred_element_type=F32)
            return total + jnp.sum(e, 0, keepdims=True)

        total = lax.fori_loop(lo, i + 1, value, jnp.zeros((1, 2 * BLK), F32))
        inv = 1.0 / total
        o_t = (ot[...] * inv).astype(BF).astype(F32)
        do_t = jnp.transpose(do.astype(F32))
        delta = jnp.sum(o_t * do_t, 0, keepdims=True)
        dqt[...] = jnp.zeros_like(dqt)

        def back(j, _):
            cols = pl.ds(pl.multiple_of(j * BLK, BLK), BLK)
            p = st[j - lo] * inv
            dp = lax.dot_general(v[cols, :], do, nt, preferred_element_type=F32)
            ds = (p * (dp - delta)).astype(BF)
            dv[cols, :] += lax.dot_general(p.astype(BF), do, nn, preferred_element_type=F32)
            dk[cols, :] += lax.dot_general(ds, q, nn, preferred_element_type=F32)
            dqt[...] += lax.dot_general(kt[:, cols], ds, nn, preferred_element_type=F32)
            return 0

        lax.fori_loop(lo, i + 1, back, 0)
        o = jnp.transpose(o_t).astype(BF)
        dq = jnp.transpose(dqt[...]) * SCALE
        new = []
        for h in range(2):
            g = unrope(dq[h * BLK : (h + 1) * BLK], c, s).astype(BF)
            new.append(carry[h] + jnp.sum(g.astype(F32), 0, keepdims=True))
            for a in range(per):
                part = slice(a * 128, (a + 1) * 128)
                out[i * per + a, 0:128, h * HEAD : (h + 1) * HEAD] = o[h * BLK + a * 128 : h * BLK + (a + 1) * 128]
                out[i * per + a, 0:128, 256 + h * HEAD : 256 + (h + 1) * HEAD] = g[part]
        for a in range(per):
            heads_out(i * per + a).start()
        return tuple(new)

    zero = jnp.zeros((1, HEAD), F32)
    head_sums = lax.fori_loop(0, blocks, block, (zero, zero))
    def wait_heads(d, _):
        heads_out(d).wait()
        return 0

    def wait_pairs(d, _):
        pair_out(d).wait()
        return 0

    if not last:
        sums[...] = jnp.zeros_like(sums)
        sums[0:1, :] = head_sums[0]
        sums[1:2, :] = head_sums[1]
        for copy in saves:
            copy.wait()
        lax.fori_loop(0, n // 128, wait_heads, 0)
        return
    for copy in old:
        copy.wait()

    def finish(b, carry):
        rows = pl.ds(pl.multiple_of(b * 128, 128), 128)
        gk = unrope((dk[rows, :] + dk_old[rows, :]) * SCALE, cos[rows, :], sin[rows, :])
        gv = dv[rows, :] + dv_old[rows, :]
        out[b, 0:128, 512:640] = gk.astype(BF)
        out[b, 0:128, 640:768] = gv.astype(BF)
        pair_out(b).start()
        return (
            carry[0] + jnp.sum(gk, 0, keepdims=True),
            carry[1] + jnp.sum(gv, 0, keepdims=True),
        )

    kv_sums = lax.fori_loop(0, n // 128, finish, (zero, zero))
    sums[...] = sums_in[...]
    sums[2:3, :] = head_sums[0]
    sums[3:4, :] = head_sums[1]
    sums[4:5, :] = kv_sums[0]
    sums[5:6, :] = kv_sums[1]
    lax.fori_loop(0, n // 128, wait_heads, 0)
    lax.fori_loop(0, n // 128, wait_pairs, 0)


def attend(last, ways, first_block, page, recv, cos, sin, first, bias, keys=(), state=()):
    n = recv.shape[0]
    width = 768 if last else 512
    grad = jax.ShapeDtypeStruct((n, HEAD), F32)
    row = jax.ShapeDtypeStruct((n, HEAD), BF)
    col = jax.ShapeDtypeStruct((HEAD, n), BF)
    sums = jax.ShapeDtypeStruct((8, HEAD), F32)
    out = jax.ShapeDtypeStruct((ways, n // ways, width), BF)
    held = [pltpu.VMEM((n, HEAD), BF)] * 2 + [pltpu.VMEM((HEAD, n), BF)] * 2 + [pltpu.VMEM((n, HEAD), F32)] * 2
    if last:
        dk, dv, old_sums = state
        args = (first_block, page, recv, *keys, cos, sin, dk, dv, first, bias, old_sums)
        in_specs = [SM, SM] + [HBM] * 9 + [VM] * 3
        outs, out_specs = (out, sums), (HBM, VM)
        held += [pltpu.VMEM((n, HEAD), F32)] * 4
    else:
        args = (first_block, page, recv, cos, sin, first, bias)
        in_specs = [SM, SM, HBM, HBM, HBM, VM, VM]
        outs = (out, row, row, col, col, grad, grad, sums)
        out_specs = (HBM,) * 5 + (VM,) * 3
        held += [pltpu.VMEM((n, 256), BF)]
    sems = [pltpu.SemaphoreType.DMA((5,)), pltpu.SemaphoreType.DMA((4,))]
    if last:
        sems.append(pltpu.SemaphoreType.DMA((2,)))
    sems.append(pltpu.SemaphoreType.DMA((ways, 2)))
    return pl.pallas_call(
        functools.partial(attend_kernel, last),
        out_shape=outs,
        in_specs=in_specs,
        out_specs=out_specs,
        scratch_shapes=held
        + [
            pltpu.VMEM((n, 256), BF),
            pltpu.VMEM((n, 256), BF),
            pltpu.VMEM((1024 // BLK + 1, BLK, 2 * BLK), F32),
            pltpu.VMEM((HEAD, 2 * BLK), F32),
            pltpu.VMEM((HEAD, 2 * BLK), F32),
            pltpu.VMEM((ways, n // ways, width), BF),
        ]
        + sems,
        compiler_params=params(60),
        cost_estimate=cost(20 * 10**9, 10**7),
        name="attend1" if last else "attend0",
    )(*args)


def head_copies(recv, att, gq, chunk, sem):
    copies = []
    for d in range(recv.shape[0]):
        cols = pl.ds(d * 512 + chunk * 256, 256)
        rows = pl.ds(0, 128)
        copies.append(pltpu.make_async_copy(recv.at[d, rows, pl.ds(0, 256)], att.at[:, cols], sem.at[d, 0]))
        copies.append(pltpu.make_async_copy(recv.at[d, rows, pl.ds(256, 256)], gq.at[:, cols], sem.at[d, 1]))
    return copies


def unpack0_kernel(recv, att, gq, sem):
    run_copies(head_copies(recv, att, gq, 0, sem))


def unpack0(recv):
    ways, rows, _ = recv.shape
    shape = jax.ShapeDtypeStruct((rows, QUERY_HEADS * HEAD), BF)
    return pl.pallas_call(
        unpack0_kernel,
        out_shape=(shape, shape),
        in_specs=[VM],
        out_specs=(ANY, ANY),
        scratch_shapes=[pltpu.SemaphoreType.DMA((ways, 2))],
        compiler_params=params(60),
        cost_estimate=cost(0, 4 * ways * rows * 512),
        name="unpack0",
    )(recv)


def unpack1_kernel(place, recv, s0, s1, s2, s3, _a, _g, att, gq, kvg, gb, sem):
    copies = head_copies(recv, att, gq, 1, sem)
    for copy in copies:
        copy.start()
    share = recv.shape[0] // KEY_VALUE_HEADS
    kw = KEY_VALUE_HEADS * HEAD
    gb[QUERY_HEADS:, :] = jnp.zeros((2 * KEY_VALUE_HEADS, HEAD), F32)
    for ky, piece in enumerate((s0, s1, s2, s3)):
        for kx in range(SIDE):
            owner = lax.rem(place[1] + SIDE - ky, SIDE) * SIDE + lax.rem(place[0] + SIDE - kx, SIDE)
            part = piece[kx]
            for h in range(4):
                gb[pl.ds(owner * 4 + h, 1), :] = part[h : h + 1, :]
            head = owner // share
            gb[pl.ds(QUERY_HEADS + head, 1), :] += part[4:5, :]
            gb[pl.ds(QUERY_HEADS + KEY_VALUE_HEADS + head, 1), :] += part[5:6, :]
    for h in range(KEY_VALUE_HEADS):
        grad = jnp.zeros((128, 256), F32)
        for r in range(share):
            grad = grad + recv[h * share + r, :, 512:768].astype(F32)
        kvg[:, h * HEAD : (h + 1) * HEAD] = grad[:, :HEAD].astype(BF)
        kvg[:, kw + h * HEAD : kw + (h + 1) * HEAD] = grad[:, HEAD:].astype(BF)
    for copy in copies:
        copy.wait()


def unpack1(place, recv, pieces, att, gq):
    ways = recv.shape[0]
    rows = att.shape[0]
    return pl.pallas_call(
        unpack1_kernel,
        out_shape=(
            jax.ShapeDtypeStruct(att.shape, BF),
            jax.ShapeDtypeStruct(gq.shape, BF),
            jax.ShapeDtypeStruct((rows, 2 * KEY_VALUE_HEADS * HEAD), BF),
            jax.ShapeDtypeStruct((QUERY_HEADS + 2 * KEY_VALUE_HEADS, HEAD), F32),
        ),
        in_specs=[SM, VM, VM, VM, VM, VM, HBM, HBM],
        out_specs=(HBM, HBM, VM, VM),
        input_output_aliases={6: 0, 7: 1},
        scratch_shapes=[pltpu.SemaphoreType.DMA((ways, 2))],
        compiler_params=params(8),
        cost_estimate=cost(0, 4 * ways * rows * 768),
        name="unpack1",
    )(place, recv, *pieces, att, gq)


def shift(dx, dy):
    side = range(SIDE)
    return [(y * SIDE + x, (y + dy) % SIDE * SIDE + (x + dx) % SIDE) for y in side for x in side]


def rope_tables(positions):
    lane = jnp.arange(HEAD, dtype=jnp.int32)
    exponent = (lane % (HEAD // 2)).astype(F32) * 2.0 / HEAD
    frequency = jnp.power(jnp.float32(ROPE_BASE), -exponent)
    angles = positions.astype(F32)[:, None] * frequency[None, :]
    sign = jnp.where(lane < HEAD // 2, -1.0, 1.0).astype(F32)
    return jnp.cos(angles), jnp.sin(angles) * sign[None, :]


def exchange(x):
    return lax.all_to_all(x, "sp", split_axis=0, concat_axis=0, tiled=True)


def shards(projected, bias, cotangent, lengths, page_source):
    ways = lax.axis_size("sp")
    me = lax.axis_index("sp")
    rows = projected.shape[0]
    n = rows * ways
    page = page_source[0]
    recv0 = exchange(pack(0, ways, projected, cotangent))
    recv1 = exchange(pack(1, ways, projected, cotangent))

    ends = jnp.cumsum(lengths[0])
    starts = ends - lengths[0]
    tokens = jnp.arange(n, dtype=jnp.int32)
    first = jnp.max(jnp.where(tokens[:, None] >= starts[None, :], starts[None, :], 0), 1)
    first_block = first.reshape(n // BLK, BLK)[:, 0] // BLK
    cos, sin = rope_tables(tokens - first)
    first = first[None, :]

    share = ways // KEY_VALUE_HEADS
    kv_head = me // share
    bias_rows = bias.reshape(-1, HEAD)
    qbias = lax.dynamic_slice_in_dim(bias_rows, me * 4, 4)
    kbias = lax.dynamic_slice_in_dim(bias_rows, QUERY_HEADS + kv_head, 1)
    vbias = lax.dynamic_slice_in_dim(bias_rows, QUERY_HEADS + KEY_VALUE_HEADS + kv_head, 1)
    bias0 = jnp.concatenate([qbias[0:2], kbias, vbias], 0)

    send2, k, v, kt, vt, dk, dv, sums = attend(
        False, ways, first_block, page, recv0.reshape(n, 768), cos, sin, first, bias0
    )
    recv2 = exchange(send2)
    send3, sums = attend(
        True, ways, first_block, page, recv1.reshape(n, 512), cos, sin, first, qbias[2:4],
        (k, v, kt, vt), (dk, dv, sums),
    )
    recv3 = exchange(send3)
    sums = lax.psum(sums, "dp")
    row = jnp.stack([sums] + [lax.ppermute(sums, "sp", shift(k, 0)) for k in range(1, SIDE)])
    pieces = [row] + [lax.ppermute(row, "sp", shift(0, k)) for k in range(1, SIDE)]
    att, gq = unpack0(recv2)
    place = jnp.stack([me % SIDE, me // SIDE]).astype(jnp.int32)
    att, gq, kvg, gb = unpack1(place, recv3, pieces, att, gq)
    return att, gq, kvg, gb.reshape(-1)


def solution(mesh):
    in_specs = (P(("dp", "sp"), None), P(), P(("dp", "sp"), None), P("dp", None), P("dp", None))
    out_specs = (P(("dp", "sp"), None), P(("dp", "sp"), None), P(("dp", "sp"), None), P())
    return jax.shard_map(shards, mesh=mesh, in_specs=in_specs, out_specs=out_specs, check_vma=False)
```

```python
import functools

import jax
import jax.numpy as jnp
from jax import lax
from jax.experimental import pallas as pl
from jax.experimental.pallas import tpu as pltpu
from jax.sharding import PartitionSpec as P

QUERY_HEADS = 64
KEY_VALUE_HEADS = 8
HEAD = 128
PAGE = 16
BLK = 256
SCALE = HEAD ** (-0.5)
LOG2E = 1.4426950408889634
NEG = -1e30
ROPE_BASE = 1000000.0
SIDE = 4

BF = jnp.bfloat16
F32 = jnp.float32
ANY = pl.BlockSpec(memory_space=pl.ANY)
HBM = pl.BlockSpec(memory_space=pltpu.HBM)
VM = pl.BlockSpec(memory_space=pltpu.VMEM)
SM = pl.BlockSpec(memory_space=pltpu.SMEM)


def params(mib):
    return pltpu.CompilerParams(vmem_limit_bytes=mib * 1024 * 1024)


def cost(flops, nbytes):
    return pl.CostEstimate(flops=flops, bytes_accessed=nbytes, transcendentals=0)


def run_copies(copies):
    for copy in copies:
        copy.start()
    for copy in copies:
        copy.wait()


def pack_kernel(chunk, ways, proj, cot, out, buf, sem, out_sem):
    kv0 = QUERY_HEADS * HEAD
    copies_of = ways // KEY_VALUE_HEADS
    fetch = []
    for d in range(ways):
        col = d * 512 + chunk * 256
        moves = [
            (proj.at[:, pl.ds(col, 256)], buf.at[d, :, pl.ds(0, 256)]),
            (cot.at[:, pl.ds(col, 256)], buf.at[d, :, pl.ds(512 if chunk == 0 else 256, 256)]),
        ]
        if chunk == 0:
            kcol = kv0 + (d // copies_of) * HEAD
            vcol = kcol + KEY_VALUE_HEADS * HEAD
            moves.append((proj.at[:, pl.ds(kcol, HEAD)], buf.at[d, :, pl.ds(256, HEAD)]))
            moves.append((proj.at[:, pl.ds(vcol, HEAD)], buf.at[d, :, pl.ds(384, HEAD)]))
        fetch.append([pltpu.make_async_copy(x, y, sem.at[d, m]) for m, (x, y) in enumerate(moves)])
    for group in fetch:
        for copy in group:
            copy.start()
    stores = []
    for d in range(ways):
        for copy in fetch[d]:
            copy.wait()
        stores.append(pltpu.make_async_copy(buf.at[d], out.at[d], out_sem.at[d]))
        stores[-1].start()
    for copy in stores:
        copy.wait()


def pack(chunk, ways, proj, cot):
    rows = proj.shape[0]
    width = 768 if chunk == 0 else 512
    return pl.pallas_call(
        functools.partial(pack_kernel, chunk, ways),
        out_shape=jax.ShapeDtypeStruct((ways, rows, width), BF),
        in_specs=[ANY, ANY],
        out_specs=ANY,
        scratch_shapes=[
            pltpu.VMEM((ways, rows, width), BF),
            pltpu.SemaphoreType.DMA((ways, 4)),
            pltpu.SemaphoreType.DMA((ways,)),
        ],
        compiler_params=params(60),
        cost_estimate=cost(0, 4 * ways * rows * width),
        name=f"pack{chunk}",
    )(proj, cot)


def rope(x, c, s):
    return x * c + pltpu.roll(x, HEAD // 2, 1) * s


def unrope(g, c, s):
    return g * c - pltpu.roll(g, HEAD // 2, 1) * s


def attend_kernel(last, *refs):
    if last:
        (first_block, page, recv, k_in, v_in, kt_in, vt_in, cos_in, sin_in, dk_in, dv_in, first, bias, sums_in,
         out_hbm, sums,
         k, v, kt, vt, cos, sin, dk, dv, dk_old, dv_old, q_raw, do_raw, st, ot, dqt, out,
         sem, key_sem, grad_sem, out_sem) = refs
        loads = [(k_in, k), (v_in, v), (kt_in, kt), (vt_in, vt)]
    else:
        (first_block, page, recv, cos_in, sin_in, first, bias,
         out_hbm, k_out, v_out, kt_out, vt_out, dk, dv, sums,
         k, v, kt, vt, cos, sin, q_raw, do_raw, st, ot, dqt, out,
         sem, key_sem, out_sem) = refs
        loads = []
    n = recv.shape[0]
    blocks = n // BLK
    per = BLK // 128
    width = 256 if last else 512

    upstream = pltpu.make_async_copy(recv.at[:, pl.ds(width, 256)], do_raw, sem.at[0])
    tables = [
        pltpu.make_async_copy(cos_in, cos, sem.at[3]),
        pltpu.make_async_copy(sin_in, sin, sem.at[4]),
    ]
    keys = [pltpu.make_async_copy(x, y, key_sem.at[m]) for m, (x, y) in enumerate(loads)]

    def fetch(p, _):
        src = pl.ds(pl.multiple_of(page[p] * PAGE, PAGE), PAGE)
        dst = pl.ds(pl.multiple_of(p * PAGE, PAGE), PAGE)
        pltpu.make_async_copy(recv.at[src, pl.ds(0, width)], q_raw.at[dst, :], sem.at[1]).start()
        return 0

    for copy in tables:
        copy.start()
    lax.fori_loop(0, n // PAGE, fetch, 0, unroll=4)
    for copy in keys + [upstream]:
        copy.start()
    dk[...] = jnp.zeros_like(dk)
    dv[...] = jnp.zeros_like(dv)
    for copy in tables:
        copy.wait()
    if last:
        old = [
            pltpu.make_async_copy(dk_in, dk_old, grad_sem.at[0]),
            pltpu.make_async_copy(dv_in, dv_old, grad_sem.at[1]),
        ]
        for copy in old:
            copy.start()
        for copy in keys:
            copy.wait()
    pltpu.make_async_copy(recv.at[:, pl.ds(0, width)], q_raw, sem.at[1]).wait()
    if not last:

        def prepare(b, _):
            rows = pl.ds(pl.multiple_of(b * BLK, BLK), BLK)
            x = rope(q_raw[rows, 256 : 256 + HEAD].astype(F32) + bias[2:3, :], cos[rows, :], sin[rows, :])
            y = q_raw[rows, 256 + HEAD : 256 + 2 * HEAD].astype(F32) + bias[3:4, :]
            k[rows, :] = x.astype(BF)
            v[rows, :] = y.astype(BF)
            kt[:, rows] = jnp.transpose(x).astype(BF)
            vt[:, rows] = jnp.transpose(y).astype(BF)
            return 0

        lax.fori_loop(0, blocks, prepare, 0)
        saves = [
            pltpu.make_async_copy(x, y, key_sem.at[m])
            for m, (x, y) in enumerate([(k, k_out), (v, v_out), (kt, kt_out), (vt, vt_out)])
        ]
        for copy in saves:
            copy.start()
    upstream.wait()

    def heads_out(d):
        return pltpu.make_async_copy(
            out.at[d, :, pl.ds(0, 512)], out_hbm.at[d, :, pl.ds(0, 512)], out_sem.at[d, 0]
        )

    def pair_out(d):
        return pltpu.make_async_copy(
            out.at[d, :, pl.ds(512, 256)], out_hbm.at[d, :, pl.ds(512, 256)], out_sem.at[d, 1]
        )

    nt = (((1,), (1,)), ((), ()))
    nn = (((1,), (0,)), ((), ()))

    def block(i, carry):
        rows = pl.ds(pl.multiple_of(i * BLK, BLK), BLK)
        c, s = cos[rows, :], sin[rows, :]
        q = jnp.concatenate(
            [
                rope(q_raw[rows, h * HEAD : (h + 1) * HEAD].astype(F32) + bias[h : h + 1, :], c, s).astype(BF)
                for h in range(2)
            ],
            0,
        )
        do = jnp.concatenate([do_raw[rows, 0:128], do_raw[rows, 128:256]], 0)
        lo = first_block[i]
        start1 = first[0:1, rows]
        start = jnp.concatenate([start1, start1], 1)
        lane = lax.broadcasted_iota(jnp.int32, (1, BLK), 1) + i * BLK
        token = jnp.concatenate([lane, lane], 1)

        def score(j, m, diagonal=False):
            cols = pl.ds(pl.multiple_of(j * BLK, BLK), BLK)
            s = lax.dot_general(k[cols, :], q, nt, preferred_element_type=F32) * (SCALE * LOG2E)
            key = lax.broadcasted_iota(jnp.int32, (BLK, 2 * BLK), 0)
            keep = key >= start - j * BLK
            if diagonal:
                keep = keep & (key <= token - j * BLK)
            s = jnp.where(keep, s, NEG)
            st[j - lo] = s
            return jnp.maximum(m, jnp.max(s, 0, keepdims=True))

        m = lax.fori_loop(lo, i, score, jnp.full((1, 2 * BLK), NEG, F32))
        m = score(i, m, True)
        ot[...] = jnp.zeros_like(ot)

        def value(j, total):
            cols = pl.ds(pl.multiple_of(j * BLK, BLK), BLK)
            e = jnp.exp2(st[j - lo] - m)
            st[j - lo] = e
            ot[...] += lax.dot_general(vt[:, cols], e.astype(BF), nn, preferred_element_type=F32)
            return total + jnp.sum(e, 0, keepdims=True)

        total = lax.fori_loop(lo, i + 1, value, jnp.zeros((1, 2 * BLK), F32))
        inv = 1.0 / total
        o_t = (ot[...] * inv).astype(BF).astype(F32)
        do_t = jnp.transpose(do.astype(F32))
        delta = jnp.sum(o_t * do_t, 0, keepdims=True)
        dqt[...] = jnp.zeros_like(dqt)

        def back(j, _):
            cols = pl.ds(pl.multiple_of(j * BLK, BLK), BLK)
            p = st[j - lo] * inv
            dp = lax.dot_general(v[cols, :], do, nt, preferred_element_type=F32)
            ds = (p * (dp - delta)).astype(BF)
            dv[cols, :] += lax.dot_general(p.astype(BF), do, nn, preferred_element_type=F32)
            dk[cols, :] += lax.dot_general(ds, q, nn, preferred_element_type=F32)
            dqt[...] += lax.dot_general(kt[:, cols], ds, nn, preferred_element_type=F32)
            return 0

        lax.fori_loop(lo, i + 1, back, 0)
        o = jnp.transpose(o_t).astype(BF)
        dq = jnp.transpose(dqt[...]) * SCALE
        new = []
        for h in range(2):
            g = unrope(dq[h * BLK : (h + 1) * BLK], c, s).astype(BF)
            new.append(carry[h] + jnp.sum(g.astype(F32), 0, keepdims=True))
            for a in range(per):
                part = slice(a * 128, (a + 1) * 128)
                out[i * per + a, 0:128, h * HEAD : (h + 1) * HEAD] = o[h * BLK + a * 128 : h * BLK + (a + 1) * 128]
                out[i * per + a, 0:128, 256 + h * HEAD : 256 + (h + 1) * HEAD] = g[part]
        for a in range(per):
            heads_out(i * per + a).start()
        return tuple(new)

    zero = jnp.zeros((1, HEAD), F32)
    head_sums = lax.fori_loop(0, blocks, block, (zero, zero))
    def wait_heads(d, _):
        heads_out(d).wait()
        return 0

    def wait_pairs(d, _):
        pair_out(d).wait()
        return 0

    if not last:
        sums[...] = jnp.zeros_like(sums)
        sums[0:1, :] = head_sums[0]
        sums[1:2, :] = head_sums[1]
        for copy in saves:
            copy.wait()
        lax.fori_loop(0, n // 128, wait_heads, 0)
        return
    for copy in old:
        copy.wait()

    def finish(b, carry):
        rows = pl.ds(pl.multiple_of(b * 128, 128), 128)
        gk = unrope((dk[rows, :] + dk_old[rows, :]) * SCALE, cos[rows, :], sin[rows, :])
        gv = dv[rows, :] + dv_old[rows, :]
        out[b, 0:128, 512:640] = gk.astype(BF)
        out[b, 0:128, 640:768] = gv.astype(BF)
        pair_out(b).start()
        return (
            carry[0] + jnp.sum(gk, 0, keepdims=True),
            carry[1] + jnp.sum(gv, 0, keepdims=True),
        )

    kv_sums = lax.fori_loop(0, n // 128, finish, (zero, zero))
    sums[...] = sums_in[...]
    sums[2:3, :] = head_sums[0]
    sums[3:4, :] = head_sums[1]
    sums[4:5, :] = kv_sums[0]
    sums[5:6, :] = kv_sums[1]
    lax.fori_loop(0, n // 128, wait_heads, 0)
    lax.fori_loop(0, n // 128, wait_pairs, 0)


def attend(last, ways, first_block, page, recv, cos, sin, first, bias, keys=(), state=()):
    n = recv.shape[0]
    width = 768 if last else 512
    grad = jax.ShapeDtypeStruct((n, HEAD), F32)
    row = jax.ShapeDtypeStruct((n, HEAD), BF)
    col = jax.ShapeDtypeStruct((HEAD, n), BF)
    sums = jax.ShapeDtypeStruct((8, HEAD), F32)
    out = jax.ShapeDtypeStruct((ways, n // ways, width), BF)
    held = [pltpu.VMEM((n, HEAD), BF)] * 2 + [pltpu.VMEM((HEAD, n), BF)] * 2 + [pltpu.VMEM((n, HEAD), F32)] * 2
    if last:
        dk, dv, old_sums = state
        args = (first_block, page, recv, *keys, cos, sin, dk, dv, first, bias, old_sums)
        in_specs = [SM, SM] + [HBM] * 9 + [VM] * 3
        outs, out_specs = (out, sums), (HBM, VM)
        held += [pltpu.VMEM((n, HEAD), F32)] * 4
    else:
        args = (first_block, page, recv, cos, sin, first, bias)
        in_specs = [SM, SM, HBM, HBM, HBM, VM, VM]
        outs = (out, row, row, col, col, grad, grad, sums)
        out_specs = (HBM,) * 5 + (VM,) * 3
    sems = [pltpu.SemaphoreType.DMA((5,)), pltpu.SemaphoreType.DMA((4,))]
    if last:
        sems.append(pltpu.SemaphoreType.DMA((2,)))
    sems.append(pltpu.SemaphoreType.DMA((ways, 2)))
    return pl.pallas_call(
        functools.partial(attend_kernel, last),
        out_shape=outs,
        in_specs=in_specs,
        out_specs=out_specs,
        scratch_shapes=held
        + [
            pltpu.VMEM((n, 256 if last else 512), BF),
            pltpu.VMEM((n, 256), BF),
            pltpu.VMEM((1024 // BLK + 1, BLK, 2 * BLK), F32),
            pltpu.VMEM((HEAD, 2 * BLK), F32),
            pltpu.VMEM((HEAD, 2 * BLK), F32),
            pltpu.VMEM((ways, n // ways, width), BF),
        ]
        + sems,
        compiler_params=params(60),
        cost_estimate=cost(20 * 10**9, 10**7),
        name="attend1" if last else "attend0",
    )(*args)


def head_copies(recv, att, gq, chunk, sem):
    copies = []
    for d in range(recv.shape[0]):
        cols = pl.ds(d * 512 + chunk * 256, 256)
        rows = pl.ds(0, 128)
        copies.append(pltpu.make_async_copy(recv.at[d, rows, pl.ds(0, 256)], att.at[:, cols], sem.at[d, 0]))
        copies.append(pltpu.make_async_copy(recv.at[d, rows, pl.ds(256, 256)], gq.at[:, cols], sem.at[d, 1]))
    return copies


def unpack0_kernel(recv, att, gq, sem):
    run_copies(head_copies(recv, att, gq, 0, sem))


def unpack0(recv):
    ways, rows, _ = recv.shape
    shape = jax.ShapeDtypeStruct((rows, QUERY_HEADS * HEAD), BF)
    return pl.pallas_call(
        unpack0_kernel,
        out_shape=(shape, shape),
        in_specs=[VM],
        out_specs=(ANY, ANY),
        scratch_shapes=[pltpu.SemaphoreType.DMA((ways, 2))],
        compiler_params=params(60),
        cost_estimate=cost(0, 4 * ways * rows * 512),
        name="unpack0",
    )(recv)


def unpack1_kernel(place, recv, *refs):
    ways = recv.shape[0]
    pieces = refs[:ways]
    _a, _g, att, gq, kvg, gb, sem = refs[ways:]
    copies = head_copies(recv, att, gq, 1, sem)
    for copy in copies:
        copy.start()
    share = recv.shape[0] // KEY_VALUE_HEADS
    kw = KEY_VALUE_HEADS * HEAD
    gb[QUERY_HEADS:, :] = jnp.zeros((2 * KEY_VALUE_HEADS, HEAD), F32)
    for ky in range(SIDE):
        for kx in range(SIDE):
            owner = lax.rem(place[1] + SIDE - ky, SIDE) * SIDE + lax.rem(place[0] + SIDE - kx, SIDE)
            part = pieces[ky * SIDE + kx]
            for h in range(4):
                gb[pl.ds(owner * 4 + h, 1), :] = part[h : h + 1, :]
            head = owner // share
            gb[pl.ds(QUERY_HEADS + head, 1), :] += part[4:5, :]
            gb[pl.ds(QUERY_HEADS + KEY_VALUE_HEADS + head, 1), :] += part[5:6, :]
    for h in range(KEY_VALUE_HEADS):
        grad = jnp.zeros((128, 256), F32)
        for r in range(share):
            grad = grad + recv[h * share + r, :, 512:768].astype(F32)
        kvg[:, h * HEAD : (h + 1) * HEAD] = grad[:, :HEAD].astype(BF)
        kvg[:, kw + h * HEAD : kw + (h + 1) * HEAD] = grad[:, HEAD:].astype(BF)
    for copy in copies:
        copy.wait()


def unpack1(place, recv, pieces, att, gq):
    ways = recv.shape[0]
    rows = att.shape[0]
    return pl.pallas_call(
        unpack1_kernel,
        out_shape=(
            jax.ShapeDtypeStruct(att.shape, BF),
            jax.ShapeDtypeStruct(gq.shape, BF),
            jax.ShapeDtypeStruct((rows, 2 * KEY_VALUE_HEADS * HEAD), BF),
            jax.ShapeDtypeStruct((QUERY_HEADS + 2 * KEY_VALUE_HEADS, HEAD), F32),
        ),
        in_specs=[SM] + [VM] * (1 + ways) + [HBM, HBM],
        out_specs=(HBM, HBM, VM, VM),
        input_output_aliases={2 + ways: 0, 3 + ways: 1},
        scratch_shapes=[pltpu.SemaphoreType.DMA((ways, 2))],
        compiler_params=params(8),
        cost_estimate=cost(0, 4 * ways * rows * 768),
        name="unpack1",
    )(place, recv, *pieces, att, gq)


def shift(dx, dy):
    side = range(SIDE)
    return [(y * SIDE + x, (y + dy) % SIDE * SIDE + (x + dx) % SIDE) for y in side for x in side]


def rope_tables(positions):
    lane = jnp.arange(HEAD, dtype=jnp.int32)
    exponent = (lane % (HEAD // 2)).astype(F32) * 2.0 / HEAD
    frequency = jnp.power(jnp.float32(ROPE_BASE), -exponent)
    angles = positions.astype(F32)[:, None] * frequency[None, :]
    sign = jnp.where(lane < HEAD // 2, -1.0, 1.0).astype(F32)
    return jnp.cos(angles), jnp.sin(angles) * sign[None, :]


def exchange(x):
    return lax.all_to_all(x, "sp", split_axis=0, concat_axis=0, tiled=True)


def shards(projected, bias, cotangent, lengths, page_source):
    ways = lax.axis_size("sp")
    me = lax.axis_index("sp")
    rows = projected.shape[0]
    n = rows * ways
    page = page_source[0]
    recv0 = exchange(pack(0, ways, projected, cotangent))
    recv1 = exchange(pack(1, ways, projected, cotangent))

    ends = jnp.cumsum(lengths[0])
    starts = ends - lengths[0]
    tokens = jnp.arange(n, dtype=jnp.int32)
    first = jnp.max(jnp.where(tokens[:, None] >= starts[None, :], starts[None, :], 0), 1)
    first_block = first.reshape(n // BLK, BLK)[:, 0] // BLK
    cos, sin = rope_tables(tokens - first)
    first = first[None, :]

    share = ways // KEY_VALUE_HEADS
    kv_head = me // share
    bias_rows = bias.reshape(-1, HEAD)
    qbias = lax.dynamic_slice_in_dim(bias_rows, me * 4, 4)
    kbias = lax.dynamic_slice_in_dim(bias_rows, QUERY_HEADS + kv_head, 1)
    vbias = lax.dynamic_slice_in_dim(bias_rows, QUERY_HEADS + KEY_VALUE_HEADS + kv_head, 1)
    bias0 = jnp.concatenate([qbias[0:2], kbias, vbias], 0)

    send2, k, v, kt, vt, dk, dv, sums = attend(
        False, ways, first_block, page, recv0.reshape(n, 768), cos, sin, first, bias0
    )
    recv2 = exchange(send2)
    send3, sums = attend(
        True, ways, first_block, page, recv1.reshape(n, 512), cos, sin, first, qbias[2:4],
        (k, v, kt, vt), (dk, dv, sums),
    )
    recv3 = exchange(send3)
    sums = lax.psum(sums, "dp")
    pieces = [
        lax.ppermute(sums, "sp", shift(kx, ky)) if kx or ky else sums for ky in range(SIDE) for kx in range(SIDE)
    ]
    att, gq = unpack0(recv2)
    place = jnp.stack([me % SIDE, me // SIDE]).astype(jnp.int32)
    att, gq, kvg, gb = unpack1(place, recv3, pieces, att, gq)
    return att, gq, kvg, gb.reshape(-1)


def solution(mesh):
    in_specs = (P(("dp", "sp"), None), P(), P(("dp", "sp"), None), P("dp", None), P("dp", None))
    out_specs = (P(("dp", "sp"), None), P(("dp", "sp"), None), P(("dp", "sp"), None), P())
    return jax.shard_map(shards, mesh=mesh, in_specs=in_specs, out_specs=out_specs, check_vma=False)
```
